32 devices in a mesh: lat: 4 (over x, core), lon: 8 (over z, y).
Axes of the slice: x: 2, y: 2, z: 4, core: 2. Of those that a mesh axis runs over, the one named last changes fastest.
Arguments:
- tokens: bfloat16 [64, 128, 1024], P('lat', 'lon'), may hold values from -6 to 6
- norm_gain: float32 [1024], replicated, may hold values from 0.25 to 1.75
- w_qkv: bfloat16 [1024, 3072], replicated, may hold values from -0.1875 to 0.1875
- w_out: bfloat16 [1024, 1024], replicated, may hold values from -0.1875 to 0.1875
- cotangent: bfloat16 [64, 128, 1024], P('lat', 'lon'), may hold values from -6 to 6
Outputs:
- result: bfloat16 [64, 128, 1024], P('lat', 'lon')
- grad_tokens: bfloat16 [64, 128, 1024], P('lat', 'lon')
- grad_w_qkv: float32 [1024, 3072], P(('lat', 'lon'))
- grad_w_out: float32 [1024, 1024], P(('lat', 'lon'))
The draws below stay inside these ranges and needn't reach their ends.
All inputs are finite; a program needn't handle non-finite values.
Results may differ from the reference program's by a relative error of at most 0.025.
Values may be sent and summed in bfloat16 or wider, within the bound.
A program may use at most 192 MiB of HBM per device.

```python
import jax
import jax.numpy as jnp
from jax import lax

D = 1024
H = 16
R = 6
NLAT = 64
NLON = 128


def spiked(entries, stream_key, source, target, shards_of, factor):
    def block_of(dim):
        return (jnp.arange(entries.shape[dim]) // (entries.shape[dim] // shards_of)).reshape((-1,) + (1,) * (entries.ndim - 1 - dim))

    near = jax.random.permutation(stream_key, shards_of)[block_of(target)]
    far = (block_of(target) + shards_of // 2) % shards_of
    return jnp.where((block_of(source) == near) | (block_of(source) == far), factor * entries, entries)


def steps_of(own_key, shape, cuts, smallest, largest):
    def one(dim, blocks):
        heights = jax.random.uniform(jax.random.fold_in(jax.random.fold_in(own_key, 6), dim), (blocks,), jnp.float32, smallest / len(cuts), largest / len(cuts))
        return jnp.repeat(jnp.exp(heights), shape[dim] // blocks).reshape((-1,) + (1,) * (len(shape) - dim - 1))

    loudness = one(*cuts[0])
    for cut in cuts[1:]:
        loudness = loudness * one(*cut)
    return loudness


def centred(stream_key, shape, width, bound, split=(), dtype=jnp.bfloat16):
    drawn = jax.random.normal(stream_key, shape, jnp.float32) * width
    if len(split) > 0:
        drawn = steps_of(stream_key, shape, split, -0.22, 0.18) * drawn
    return jnp.clip(drawn, min=-bound, max=bound).astype(dtype)


def heavy_noise(stream_key, extent, width, reach, pieces, heavy, held_as=jnp.bfloat16):
    values = width * jax.random.normal(stream_key, extent, jnp.float32)
    if pieces:
        values = values * steps_of(stream_key, extent, pieces, -0.22, 0.18)
    return jnp.clip(spiked(values, jax.random.fold_in(stream_key, 3), *heavy), -reach, reach).astype(held_as)


def setup_inputs(seed: int = 0) -> dict:
    arg_keys = jax.random.split(jax.random.key(seed), 6)
    return {
        "tokens": heavy_noise(arg_keys[0], (NLAT, NLON, D), 1.0, 6.0, ((0, 4), (1, 8)), (1, 2, 8, 2.0)),
        "norm_gain": jnp.clip(1.0 + 0.15 * jax.random.normal(arg_keys[1], (D,), jnp.float32), 0.25, 1.75),
        "w_qkv": centred(arg_keys[2], (D, 3 * D), D ** -0.5, 0.1875),
        "w_out": centred(arg_keys[3], (D, D), D ** -0.5, 0.1875),
        "cotangent": centred(arg_keys[4], (NLAT, NLON, D), 1.0, 6.0, ((0, 4), (1, 8))),
    }


epsilon = 1e-06

def extend(values):
    turned = jnp.roll(values, NLON // 2, axis=1)
    north_rows = turned[:R][::-1]
    south_rows = turned[NLAT - R:][::-1]
    stacked = jnp.concatenate([north_rows, values, south_rows], axis=0)
    return jnp.concatenate([stacked[:, NLON - R:], stacked, stacked[:, :R]], axis=1)

def shifted(stripe, offset):
    line = lax.dynamic_index_in_dim(stripe, offset, 0, keepdims=False)
    return jnp.stack([line[column:column + NLON] for column in range(2 * R + 1)])

def heads_of(values):
    return values.astype(jnp.float32).reshape(values.shape[:-1] + (H, D // H))

def rounded(values):
    return lax.optimization_barrier(values.astype(jnp.bfloat16)).astype(jnp.float32)

def offsets_list():
    return jnp.arange(2 * R + 1).astype(jnp.int32)

def forward_row(row_index, queries, keys_ext, values_ext):
    factor = (D // H) ** (-0.5)
    centre = heads_of(queries[row_index])
    key_stripe = lax.dynamic_slice_in_dim(keys_ext, row_index, 2 * R + 1, 0)
    value_stripe = lax.dynamic_slice_in_dim(values_ext, row_index, 2 * R + 1, 0)

    def score_line(offset):
        return jnp.einsum('nhd,bnhd->bnh', centre, heads_of(shifted(key_stripe, offset))) * factor
    scores = lax.map(score_line, offsets_list())
    highest = lax.optimization_barrier(jnp.max(scores, axis=(0, 1)))
    log_total = highest + jnp.log(lax.optimization_barrier(jnp.sum(jnp.exp(scores - highest), axis=(0, 1))))
    chances_low = rounded(jnp.exp(scores - log_total))

    def add_line(summed, inputs):
        offset, weights = inputs
        return (summed + jnp.einsum('bnh,bnhd->nhd', weights, heads_of(shifted(value_stripe, offset))), None)
    initial = jnp.zeros((NLON, H, D // H), jnp.float32)
    summed, unused = lax.scan(add_line, initial, (offsets_list(), chances_low))
    return (summed.reshape(NLON, D).astype(jnp.bfloat16), log_total)

def query_row(row_index, queries, grads, totals, deltas, keys_ext, values_ext):
    factor = (D // H) ** (-0.5)
    centre = heads_of(queries[row_index])
    incoming = heads_of(grads[row_index])
    row_total = totals[row_index]
    row_delta = deltas[row_index]
    key_stripe = lax.dynamic_slice_in_dim(keys_ext, row_index, 2 * R + 1, 0)
    value_stripe = lax.dynamic_slice_in_dim(values_ext, row_index, 2 * R + 1, 0)

    def add_line(summed, offset):
        keys_here = heads_of(shifted(key_stripe, offset))
        values_here = heads_of(shifted(value_stripe, offset))
        scores = jnp.einsum('nhd,bnhd->bnh', centre, keys_here) * factor
        chances = jnp.exp(scores - row_total)
        grad_chances = jnp.einsum('nhd,bnhd->bnh', incoming, values_here)
        grad_scores = rounded(chances * (grad_chances - row_delta))
        return (summed + jnp.einsum('bnh,bnhd->nhd', grad_scores, keys_here), None)
    initial = jnp.zeros((NLON, H, D // H), jnp.float32)
    summed, unused = lax.scan(add_line, initial, offsets_list())
    return (summed * factor).reshape(NLON, D)

def key_row(row_index, keys, values, queries_ext, grads_ext, totals_ext, deltas_ext):
    factor = (D // H) ** (-0.5)
    own_keys = heads_of(keys[row_index])
    own_values = heads_of(values[row_index])
    query_stripe = lax.dynamic_slice_in_dim(queries_ext, row_index, 2 * R + 1, 0)
    grad_stripe = lax.dynamic_slice_in_dim(grads_ext, row_index, 2 * R + 1, 0)
    total_stripe = lax.dynamic_slice_in_dim(totals_ext, row_index, 2 * R + 1, 0)
    delta_stripe = lax.dynamic_slice_in_dim(deltas_ext, row_index, 2 * R + 1, 0)

    def add_line(sums, offset):
        far_queries = heads_of(shifted(query_stripe, offset))
        far_grads = heads_of(shifted(grad_stripe, offset))
        far_totals = shifted(total_stripe, offset)
        far_deltas = shifted(delta_stripe, offset)
        scores = jnp.einsum('nhd,bnhd->bnh', own_keys, far_queries) * factor
        chances = jnp.exp(scores - far_totals)
        grad_chances = jnp.einsum('nhd,bnhd->bnh', own_values, far_grads)
        grad_scores = rounded(chances * (grad_chances - far_deltas))
        chances_low = rounded(chances)
        key_sum = sums[0] + jnp.einsum('bnh,bnhd->nhd', grad_scores, far_queries)
        value_sum = sums[1] + jnp.einsum('bnh,bnhd->nhd', chances_low, far_grads)
        return ((key_sum, value_sum), None)
    initial = jnp.zeros((NLON, H, D // H), jnp.float32)
    sums, unused = lax.scan(add_line, (initial, initial), offsets_list())
    return ((sums[0] * factor).reshape(NLON, D), sums[1].reshape(NLON, D))

def reference(tokens, norm_gain, w_qkv, w_out, cotangent):
    source = tokens.astype(jnp.float32)
    inverse = lax.rsqrt(lax.optimization_barrier(jnp.mean(source * source, axis=-1, keepdims=True)) + epsilon)
    normed = (source * inverse * norm_gain).astype(jnp.bfloat16)
    flat_normed = normed.reshape(-1, D)
    packed = jnp.dot(flat_normed, w_qkv, preferred_element_type=jnp.float32).astype(jnp.bfloat16)
    packed = packed.reshape(NLAT, NLON, 3 * D)
    queries = packed[..., :D]
    keys = packed[..., D:2 * D]
    values = packed[..., 2 * D:]
    keys_ext = extend(keys)
    values_ext = extend(values)
    row_indices = jnp.arange(NLAT).astype(jnp.int32)

    def forward_map(row_index):
        return forward_row(row_index, queries, keys_ext, values_ext)
    attended, totals = lax.map(forward_map, row_indices)
    attended_flat = attended.reshape(-1, D)
    grad_flat = cotangent.reshape(-1, D)
    source_flat = source.reshape(-1, D)
    mixed = jnp.dot(attended_flat, w_out, preferred_element_type=jnp.float32) + source_flat
    result = mixed.astype(jnp.bfloat16).reshape(NLAT, NLON, D)
    factor_grad = (NLAT * NLON) ** (-0.5)
    grad_w_out = jnp.dot(attended_flat.T, grad_flat, preferred_element_type=jnp.float32) * factor_grad
    grad_attended = jnp.dot(grad_flat, w_out.T, preferred_element_type=jnp.float32).astype(jnp.bfloat16)
    product = grad_attended.astype(jnp.float32) * attended_flat.astype(jnp.float32)
    deltas = product.reshape(NLAT, NLON, H, D // H).sum(axis=-1)
    grad_grid = grad_attended.reshape(NLAT, NLON, D)

    def query_map(row_index):
        return query_row(row_index, queries, grad_grid, totals, deltas, keys_ext, values_ext)
    grad_query = lax.map(query_map, row_indices)
    queries_ext = extend(queries)
    grads_ext = extend(grad_grid)
    totals_ext = extend(totals)
    deltas_ext = extend(deltas)

    def key_map(row_index):
        return key_row(row_index, keys, values, queries_ext, grads_ext, totals_ext, deltas_ext)
    grad_key, grad_value = lax.map(key_map, row_indices)
    grad_packed = jnp.concatenate([grad_query, grad_key, grad_value], axis=-1).astype(jnp.bfloat16).reshape(-1, 3 * D)
    grad_w_qkv = jnp.dot(flat_normed.T, grad_packed, preferred_element_type=jnp.float32) * factor_grad
    grad_normed = jnp.dot(grad_packed, w_qkv.T, preferred_element_type=jnp.float32)
    scaled = norm_gain * grad_normed
    inverse_flat = inverse.reshape(-1, 1)
    grad_tokens = grad_flat.astype(jnp.float32) + inverse_flat * scaled - source_flat * inverse_flat ** 3 * lax.optimization_barrier(jnp.mean(source_flat * scaled, axis=-1, keepdims=True))
    return (result, grad_tokens.astype(jnp.bfloat16).reshape(NLAT, NLON, D), grad_w_qkv, grad_w_out)
```

```python
import functools

import jax
import jax.numpy as jnp
from jax import lax
from jax.experimental import pallas as pl
from jax.experimental.pallas import tpu as pltpu
from jax.sharding import PartitionSpec as P

H = 16
R = 6
SIDE = 8
PAIR = 128
TILE_ROWS = 8
CHUNK = 512
LAT_FIRST = (0, 2, 4, 5, 7)
MESH = pl.DeviceIdType.MESH

epsilon = 1e-06
floor_score = -1e30

NT = (((1,), (1,)), ((), ()))
f32 = jnp.float32
bf16 = jnp.bfloat16


def dot(a, b, dims=(((1,), (0,)), ((), ()))):
    return lax.dot_general(a, b, dims, preferred_element_type=f32)


class Ring:
    def __init__(self, rows, cols):
        self.rows, self.cols = rows, cols
        self.row = R * cols
        self.corner = R * SIDE
        self.mid = rows * SIDE
        self.side = (rows + 2 * R) * SIDE
        self.west = 2 * self.row
        self.east = self.west + self.side
        self.size = self.east + self.side

    def pieces(self):
        found = [(-1, 0, 0, self.row), (1, 0, self.row, self.row)]
        for h, start in ((-1, self.west), (1, self.east)):
            found.append((-1, h, start, self.corner))
            found.append((0, h, start + self.corner, self.mid))
            found.append((1, h, start + self.corner + self.mid, self.corner))
        return found


def place_of(lats, lons):
    lat, lon = lax.axis_index("lat"), lax.axis_index("lon")
    return lat, lon, lat == 0, lat == lats - 1


def neighbour(lats, lons, v, h):
    lat, lon, north, south = place_of(lats, lons)
    polar = north if v < 0 else south
    if v == 0:
        return {"lat": lat, "lon": lax.rem(lon + h + lons, lons)}
    return {
        "lat": jnp.where(polar, lat, lat + v),
        "lon": lax.rem(lon + h + lons + jnp.where(polar, lons // 2, 0), lons),
    }


def ring_copies(ring, lats, lons, src, dst, send_sem, recv_sem):
    lat, lon, north, south = place_of(lats, lons)
    offsets = {(v, h): (i, at) for i, (v, h, at, length) in enumerate(ring.pieces())}
    copies = []
    for i, (v, h, at, length) in enumerate(ring.pieces()):
        slot, low = offsets[(-v, -h)]
        if v != 0:
            same_slot, same_low = offsets[(v, -h)]
            polar = north if v < 0 else south
            slot = jnp.where(polar, same_slot, slot)
            low = pl.multiple_of(jnp.where(polar, same_low, low), 16)
        copies.append(
            pltpu.make_async_remote_copy(
                src_ref=src.at[pl.ds(at, length)],
                dst_ref=dst.at[pl.ds(low, length)],
                send_sem=send_sem.at[i],
                recv_sem=recv_sem.at[slot],
                device_id=neighbour(lats, lons, v, h),
                device_id_type=MESH,
            )
        )
    return copies


def ring_arrivals(ring, lats, lons, dst, send_sem, recv_sem):
    found = []
    for i, (v, h, at, length) in enumerate(ring.pieces()):
        found.append(
            pltpu.make_async_remote_copy(
                src_ref=dst.at[pl.ds(at, length)],
                dst_ref=dst.at[pl.ds(at, length)],
                send_sem=send_sem.at[i],
                recv_sem=recv_sem.at[i],
                device_id=neighbour(lats, lons, v, h),
                device_id_type=MESH,
            )
        )
    return found


def turned(cells, polar):
    flipped = jnp.concatenate([cells[r : r + 1] for r in reversed(range(R))], axis=0)
    return jnp.where(polar, flipped, cells)


def put(ref, at, cells):
    count = cells.shape[0] * cells.shape[1]
    ref[at : at + count, :] = cells.reshape(count, cells.shape[2]).astype(bf16)


def greet(devices):
    barrier = pltpu.get_barrier_semaphore()
    for device in devices:
        pl.semaphore_signal(barrier, inc=1, device_id=device, device_id_type=MESH)
    return barrier


def project_kernel(
    ring, lats, lons,
    tok_ref, gain_ref, cot_ref, wqkv_hbm, wout_hbm,
    q_ref, ga_ref, kv_ref, nt_ref,
    stage, halo, own, wqkv, wout, load_sem, send_sem, recv_sem,
):
    rows, cols = ring.rows, ring.cols
    cells, width = tok_ref.shape
    lat, lon, north, south = place_of(lats, lons)
    around = [neighbour(lats, lons, v, h) for v, h, at, length in ring.pieces()]
    barrier = greet(around)
    load_out = pltpu.make_async_copy(wout_hbm, wout, load_sem.at[0])
    load_qkv = pltpu.make_async_copy(wqkv_hbm, wqkv, load_sem.at[1])
    load_out.start()
    load_qkv.start()

    source = tok_ref[...].astype(f32)
    inverse = lax.rsqrt(jnp.mean(source * source, axis=-1, keepdims=True) + epsilon)
    normed = source * inverse * gain_ref[...]
    own[...] = normed.astype(bf16)
    grid = normed.reshape(rows, cols, width)
    top, bottom = turned(grid[:R], north), turned(grid[rows - R :], south)
    put(stage, 0, top)
    put(stage, ring.row, bottom)
    for start, c in ((ring.west, 0), (ring.east, cols - SIDE)):
        put(stage, start, top[:, c : c + SIDE])
        put(stage, start + ring.corner, grid[:, c : c + SIDE])
        put(stage, start + ring.corner + ring.mid, bottom[:, c : c + SIDE])
    pl.semaphore_wait(barrier, len(around))
    copies = ring_copies(ring, lats, lons, stage, halo, send_sem, recv_sem)
    for copy in copies:
        copy.start()

    tile = CHUNK
    load_out.wait()
    for j in range(width // tile):
        at = slice(j * tile, (j + 1) * tile)
        ga_ref[:, at] = dot(cot_ref[...], wout[at, :], NT).astype(bf16)
    load_qkv.wait()
    for j in range(width // tile):
        at = slice(j * tile, (j + 1) * tile)
        q_ref[:, at] = dot(own[...], wqkv[:, at]).astype(bf16)

    def keyval(source_ref, low):
        count = source_ref.shape[0]

        def one(j, carry):
            into = pl.ds(pl.multiple_of(j * tile, tile), tile)
            at = pl.ds(pl.multiple_of(width + j * tile, tile), tile)
            kv_ref[low : low + count, into] = dot(source_ref[...], wqkv[:, at]).astype(bf16)
            return carry

        lax.fori_loop(0, 2 * width // tile, one, 0)

    keyval(own, 0)
    nt_ref[:, :cells] = jnp.transpose(own[...])
    for arrival in ring_arrivals(ring, lats, lons, halo, send_sem, recv_sem):
        arrival.wait_recv()
    keyval(halo, cells)
    nt_ref[:, cells:] = jnp.transpose(halo[...])
    for copy in copies:
        copy.wait_send()


def project(ring, lats, lons, tokens, gain, cotangent, w_qkv, w_out):
    cells, width = tokens.shape
    frame = cells + ring.size
    vmem = pl.BlockSpec(memory_space=pltpu.VMEM)
    anywhere = pl.BlockSpec(memory_space=pl.ANY)
    count = len(ring.pieces())
    return pl.pallas_call(
        functools.partial(project_kernel, ring, lats, lons),
        in_specs=[vmem, vmem, vmem, anywhere, anywhere],
        out_specs=[vmem] * 4,
        out_shape=[
            jax.ShapeDtypeStruct((cells, width), bf16),
            jax.ShapeDtypeStruct((cells, width), bf16),
            jax.ShapeDtypeStruct((frame, 2 * width), bf16),
            jax.ShapeDtypeStruct((width, frame), bf16),
        ],
        scratch_shapes=[
            pltpu.VMEM((ring.size, width), bf16),
            pltpu.VMEM((ring.size, width), bf16),
            pltpu.VMEM((cells, width), bf16),
            pltpu.VMEM(w_qkv.shape, bf16),
            pltpu.VMEM(w_out.shape, bf16),
            pltpu.SemaphoreType.DMA((2,)),
            pltpu.SemaphoreType.DMA((count,)),
            pltpu.SemaphoreType.DMA((count,)),
        ],
        compiler_params=pltpu.CompilerParams(
            collective_id=0, has_side_effects=True, vmem_limit_bytes=48 << 20
        ),
        cost_estimate=pl.CostEstimate(flops=6 << 30, bytes_accessed=16 << 20, transcendentals=cells),
    )(tokens, gain, cotangent, w_qkv, w_out)


def attention_kernel(ring, q_ref, k_ref, v_ref, do_ref, o_ref, ot_ref, dq_ref, dk_ref, dv_ref, mask_ref):
    rows, cols = ring.rows, ring.cols
    cells = rows * cols
    queries = TILE_ROWS * cols
    reach = TILE_ROWS + 2 * R
    mid_keys, side_keys = reach * cols, reach * SIDE
    keys = mid_keys + 2 * side_keys
    head = PAIR // 2
    tiles = rows // TILE_ROWS

    @pl.when(pl.program_id(0) == 0)
    def _():
        key = lax.broadcasted_iota(jnp.int32, (keys, 2 * queries), 0)
        query = lax.rem(lax.broadcasted_iota(jnp.int32, (keys, 2 * queries), 1), queries)
        in_mid = key < mid_keys
        in_west = key < mid_keys + side_keys
        side_key = key - jnp.where(in_west, mid_keys, mid_keys + side_keys)
        row = jnp.where(in_mid, lax.div(key, cols), lax.div(side_key, SIDE))
        col = jnp.where(
            in_mid,
            lax.rem(key, cols),
            lax.rem(side_key, SIDE) + jnp.where(in_west, -SIDE, cols),
        )
        row_gap = row - lax.div(query, cols)
        col_gap = col - lax.rem(query, cols)
        allowed = (row_gap >= 0) & (row_gap <= 2 * R) & (col_gap >= -R) & (col_gap <= R)
        mask_ref[...] = jnp.where(allowed, 0.0, floor_score)

    upper = lax.broadcasted_iota(jnp.int32, (2 * queries, PAIR), 0) < queries
    left = lax.broadcasted_iota(jnp.int32, (2 * queries, PAIR), 1) < head
    own = upper == left
    upper_t = lax.broadcasted_iota(jnp.int32, (PAIR, 2 * queries), 0) < head
    left_t = lax.broadcasted_iota(jnp.int32, (PAIR, 2 * queries), 1) < queries
    own_t = upper_t == left_t

    def paired(some):
        twice = jnp.concatenate([some, some], axis=0)
        return jnp.where(own, twice, 0.0)

    def unpaired(both):
        picked = jnp.where(own_t, both, 0.0)
        return picked[:, :queries] + picked[:, queries:]

    def spans(tile):
        first = tile * TILE_ROWS - R
        low, high = max(first, 0), min(first + reach, rows)
        found = [(low * cols, (high - low) * cols, (low - first) * cols)]
        if first < 0:
            found.append((cells, -first * cols, 0))
        if first + reach > rows:
            count = first + reach - rows
            found.append((cells + ring.row, count * cols, mid_keys - count * cols))
        side_low = cells + ring.west + tile * TILE_ROWS * SIDE
        found.append((side_low, side_keys, mid_keys))
        found.append((side_low + ring.side, side_keys, mid_keys + side_keys))
        return sorted(found, key=lambda span: span[2])

    def gathered(ref, tile):
        return jnp.concatenate([ref[at : at + n, :] for at, n, to in spans(tile)], axis=0)

    dks, dvs = [], []
    for tile in range(tiles):
        own_rows = slice(tile * queries, (tile + 1) * queries)
        k = gathered(k_ref, tile)
        v = gathered(v_ref, tile)
        k_t = jnp.transpose(k)
        v_t = jnp.transpose(v)
        q32 = q_ref[own_rows, :].astype(f32) * (head ** (-0.5))
        do32 = do_ref[own_rows, :].astype(f32)
        q_pair = paired(q32).astype(bf16)
        do_pair32 = paired(do32)
        do_pair = do_pair32.astype(bf16)
        scores = dot(k, q_pair, NT) + mask_ref[...]
        highest = jnp.max(scores, axis=0, keepdims=True)
        raised = jnp.exp(scores - highest)
        chances = raised * (1.0 / jnp.sum(raised, axis=0, keepdims=True))
        chances_low = chances.astype(bf16)
        attended_t = dot(v_t, chances_low).astype(bf16).astype(f32)
        delta = jnp.sum(attended_t * jnp.transpose(do_pair32), axis=0, keepdims=True)
        attended = unpaired(attended_t)
        ot_ref[:, own_rows] = attended.astype(bf16)
        o_ref[own_rows, :] = jnp.transpose(attended).astype(bf16)
        grad_chances = dot(v, do_pair, NT)
        grad_scores = (chances * (grad_chances - delta)).astype(bf16)
        grad_query = jnp.transpose(unpaired(dot(k_t, grad_scores)))
        dq_ref[own_rows, :] = (grad_query * (head ** (-0.5))).astype(bf16)
        dks.append(dot(grad_scores, q_pair))
        dvs.append(dot(chances_low, do_pair))

    cuts = {0, cells + ring.size}
    for tile in range(tiles):
        for at, n, to in spans(tile):
            cuts |= {at, at + n}
    cuts = sorted(cuts)
    for ref, parts in ((dk_ref, dks), (dv_ref, dvs)):
        for low, high in zip(cuts, cuts[1:]):
            summed = None
            for tile, part in enumerate(parts):
                for at, n, to in spans(tile):
                    if at <= low and high <= at + n:
                        piece = part[to + low - at : to + high - at]
                        summed = piece if summed is None else summed + piece
            ref[low:high, :] = summed.astype(bf16)


def attention(ring, query, keyval, grad_attended):
    cells, width = query.shape
    frame = keyval.shape[0]
    pairs = width // PAIR
    keys = (TILE_ROWS + 2 * R) * (ring.cols + 2 * SIDE)
    one = lambda rows, shift=0: pl.BlockSpec((rows, PAIR), lambda i: (0, i + shift))
    low = lambda rows: jax.ShapeDtypeStruct((rows, width), bf16)
    return pl.pallas_call(
        functools.partial(attention_kernel, ring),
        grid=(pairs,),
        in_specs=[one(cells), one(frame), one(frame, pairs), one(cells)],
        out_specs=[
            one(cells), pl.BlockSpec((PAIR, cells), lambda i: (i, 0)), one(cells), one(frame), one(frame)
        ],
        out_shape=[low(cells), jax.ShapeDtypeStruct((width, cells), bf16), low(cells), low(frame), low(frame)],
        scratch_shapes=[pltpu.VMEM((keys, 2 * TILE_ROWS * ring.cols), f32)],
        compiler_params=pltpu.CompilerParams(vmem_limit_bytes=40 << 20),
        cost_estimate=pl.CostEstimate(
            flops=24 * cells * keys * width, bytes_accessed=16 << 20, transcendentals=cells * keys * H
        ),
    )(query, keyval, keyval, grad_attended)


def finish_kernel(
    ring, lats, lons, scale,
    tok_ref, gain_ref, cot_ref, att_ref, att_t_ref, gq_ref, gk_ref, gv_ref, nt_ref, wqkv_hbm, wout_hbm,
    result_ref, gtok_ref, gqkv_ref, gout_ref,
    stage, back, spread, wqkv, wout,
    send0, came0, send1, came1, keep1, send2, came2, keep2, send3, came3, keep3,
    load_sem, ring_send, ring_recv, s0s, s0r, s1s, s1r, s2s, s2r, s3s, s3r,
):
    rows, cols = ring.rows, ring.cols
    cells, width = tok_ref.shape
    lat, lon, north, south = place_of(lats, lons)
    hi, lo = lax.div(lat, 2), lax.rem(lat, 2)
    group, bit = lax.div(lon, 2), lax.rem(lon, 2)
    groups = lons // 2
    share = width // (lats * lons)
    block = width // lats
    chunks = 4 * width // CHUNK
    own_hi, other_hi = hi, 1 - hi
    sibling = {"lat": 2 * hi + 1 - lo, "lon": lon}
    across_lat = {"lat": 2 * (1 - hi) + lo, "lon": lon}
    across_lon = {"lat": lat, "lon": 2 * group + 1 - bit}
    along = [{"lat": lat, "lon": 2 * lax.rem(group + k, groups) + bit} for k in range(1, groups)]
    around = [neighbour(lats, lons, v, h) for v, h, at, length in ring.pieces()]
    greeted = around + [sibling, across_lat, across_lon] + along
    barrier = greet(greeted)
    load_qkv = pltpu.make_async_copy(wqkv_hbm, wqkv, load_sem.at[0])
    load_out = pltpu.make_async_copy(wout_hbm, wout, load_sem.at[1])
    load_qkv.start()
    load_out.start()
    per = width // CHUNK

    def term(half, side, c):
        low = pl.multiple_of((2 * half + side) * block, block)
        at = slice(c % per * CHUNK, (c % per + 1) * CHUNK)
        kind = c // per
        if kind == 0:
            return dot(att_t_ref[pl.ds(low, block), :], cot_ref[:, at])
        if kind == 1:
            return dot(nt_ref[pl.ds(low, block), :cells], gq_ref[:, at])
        return dot(nt_ref[pl.ds(low, block), :], (gk_ref if kind == 2 else gv_ref)[:, at])

    def remote(src, dst, send_sem, recv_sem, device):
        return pltpu.make_async_remote_copy(
            src_ref=src, dst_ref=dst, send_sem=send_sem, recv_sem=recv_sem,
            device_id=device, device_id_type=MESH,
        )

    split = lambda value: value.reshape(groups, 2, share, CHUNK)
    copy0 = [remote(send0.at[c], came0.at[c], s0s.at[c], s0r.at[c], sibling) for c in range(chunks)]
    copy1 = [
        remote(send1.at[c], came1.at[c], s1s.at[c], s1r.at[c], across_lat if c in LAT_FIRST else across_lon)
        for c in range(chunks)
    ]
    copy2 = [
        remote(send2.at[c], came2.at[c], s2s.at[c], s2r.at[c], across_lon if c in LAT_FIRST else across_lat)
        for c in range(chunks)
    ]
    copy3 = [
        [
            remote(send3.at[c, k], came3.at[c, k], s3s.at[c, k], s3r.at[c, k], along[k])
            for k in range(groups - 1)
        ]
        for c in range(chunks)
    ]

    def step0(c):
        for half in range(2):
            send0[c, half] = term(half, 1 - lo, c).astype(bf16)
        copy0[c].start()

    def step1(c):
        copy0[c].wait_recv()
        if c in LAT_FIRST:
            for half, ref, kind in ((other_hi, send1, bf16), (own_hi, keep1, f32)):
                value = split(term(half, lo, c) + came0[c, half].astype(f32))
                for second in range(2):
                    ref[c, second] = value[:, second].astype(kind)
                if ref is send1:
                    copy1[c].start()
        else:
            for half in range(2):
                value = split(term(half, lo, c) + came0[c, half].astype(f32))
                first = bit == 0
                send1[c, half] = jnp.where(first, value[:, 1], value[:, 0]).astype(bf16)
                keep1[c, half] = jnp.where(first, value[:, 0], value[:, 1])
            copy1[c].start()

    def step2(c):
        copy1[c].wait_recv()
        mine = bit if c in LAT_FIRST else hi
        send2[c] = (keep1[c, 1 - mine] + came1[c, 1 - mine].astype(f32)).astype(bf16)
        copy2[c].start()
        keep2[c] = keep1[c, mine] + came1[c, mine].astype(f32)

    def step3(c):
        copy2[c].wait_recv()
        for k in range(groups - 1):
            to = lax.rem(group + k + 1, groups)
            send3[c, k] = (keep2[c, to] + came2[c, to].astype(f32)).astype(bf16)
            copy3[c][k].start()
        keep3[c] = keep2[c, group] + came2[c, group].astype(f32)

    def step4(c):
        total = keep3[c]
        for k in range(groups - 1):
            copy3[c][k].wait_recv()
            total = total + came3[c, k].astype(f32)
        if c < per:
            gout_ref[:, c * CHUNK : (c + 1) * CHUNK] = total * scale
        else:
            gqkv_ref[:, (c - per) * CHUNK : (c - per + 1) * CHUNK] = total * scale

    pl.semaphore_wait(barrier, len(greeted))

    def halo_back():
        load_qkv.wait()

        def one(j, carry):
            at = pl.ds(pl.multiple_of(j * CHUNK, CHUNK), CHUNK)
            part = dot(gk_ref[cells:, :], wqkv[at, width : 2 * width], NT)
            part = part + dot(gv_ref[cells:, :], wqkv[at, 2 * width :], NT)
            top = turned(part[: ring.row].reshape(R, cols, CHUNK), north)
            bottom = turned(part[ring.row : 2 * ring.row].reshape(R, cols, CHUNK), south)
            stage[: ring.row, at] = top.reshape(ring.row, CHUNK).astype(bf16)
            stage[ring.row : 2 * ring.row, at] = bottom.reshape(ring.row, CHUNK).astype(bf16)
            for start in (ring.west, ring.east):
                end = start + ring.side
                low, high = start + ring.corner, end - ring.corner
                first = turned(part[start:low].reshape(R, SIDE, CHUNK), north)
                last = turned(part[high:end].reshape(R, SIDE, CHUNK), south)
                stage[start:low, at] = first.reshape(ring.corner, CHUNK).astype(bf16)
                stage[low:high, at] = part[low:high].astype(bf16)
                stage[high:end, at] = last.reshape(ring.corner, CHUNK).astype(bf16)
            return carry

        lax.fori_loop(0, width // CHUNK, one, 0)
        copies = ring_copies(ring, lats, lons, stage, back, ring_send, ring_recv)
        for copy in copies:
            copy.start()
        return copies

    ring_sent = None
    for c in range(chunks + 1):
        if c < chunks:
            step0(c)
        if c > 0:
            step1(c - 1)
        if c == 3:
            ring_sent = halo_back()

    def own_spread(j, carry):
        at = pl.ds(pl.multiple_of(j * CHUNK, CHUNK), CHUNK)
        part = dot(gq_ref[...], wqkv[at, :width], NT)
        part = part + dot(gk_ref[:cells, :], wqkv[at, width : 2 * width], NT)
        spread[:, at] = part + dot(gv_ref[:cells, :], wqkv[at, 2 * width :], NT)
        return carry

    def own_result(j, carry):
        at = pl.ds(pl.multiple_of(j * CHUNK, CHUNK), CHUNK)
        result_ref[:, at] = (dot(att_ref[...], wout[:, at]) + tok_ref[:, at].astype(f32)).astype(bf16)
        return carry

    step2(0)
    step2(1)
    lax.fori_loop(0, width // CHUNK, own_spread, 0)
    load_out.wait()
    step2(2)
    lax.fori_loop(0, width // CHUNK, own_result, 0)
    for c in range(3, chunks + 2):
        if c < chunks:
            step2(c)
        if c - 3 < chunks:
            step3(c - 3)
    step3(chunks - 1)

    for arrival in ring_arrivals(ring, lats, lons, back, ring_send, ring_recv):
        arrival.wait_recv()
    piece = lambda at, n, m: back[at : at + n * m, :].astype(f32).reshape(n, m, width)
    both = lambda at, n: jnp.concatenate(
        [piece(ring.west + at, n, SIDE), piece(ring.east + at, n, SIDE)], axis=1
    )
    top = piece(0, R, cols) + both(0, R)
    bottom = piece(ring.row, R, cols) + both(ring.corner + ring.mid, R)
    grad = spread[...].reshape(rows, cols, width) + both(ring.corner, rows)
    grad = jnp.concatenate([grad[:R] + top, grad[R : rows - R], grad[rows - R :] + bottom], axis=0)
    scaled = gain_ref[...] * grad.reshape(cells, width)
    source = tok_ref[...].astype(f32)
    inverse = lax.rsqrt(jnp.mean(source * source, axis=-1, keepdims=True) + epsilon)
    shift = inverse**3 * jnp.mean(source * scaled, axis=-1, keepdims=True)
    gtok_ref[...] = (cot_ref[...].astype(f32) + inverse * scaled - source * shift).astype(bf16)

    for c in range(chunks):
        step4(c)
    for copy in ring_sent + copy0 + copy1 + copy2 + [copy for some in copy3 for copy in some]:
        copy.wait_send()


def finish(ring, lats, lons, scale, *operands):
    tokens = operands[0]
    w_qkv, w_out = operands[-2:]
    cells, width = tokens.shape
    chunks = 4 * width // CHUNK
    groups = lons // 2
    share = width // (lats * lons)
    block = width // lats
    vmem = pl.BlockSpec(memory_space=pltpu.VMEM)
    anywhere = pl.BlockSpec(memory_space=pl.ANY)
    count = len(ring.pieces())
    sems = lambda *shape: pltpu.SemaphoreType.DMA(shape)
    return pl.pallas_call(
        functools.partial(finish_kernel, ring, lats, lons, scale),
        in_specs=[vmem] * (len(operands) - 2) + [anywhere] * 2,
        out_specs=[vmem] * 4,
        out_shape=[
            jax.ShapeDtypeStruct((cells, width), bf16),
            jax.ShapeDtypeStruct((cells, width), bf16),
            jax.ShapeDtypeStruct((share, 3 * width), f32),
            jax.ShapeDtypeStruct((share, width), f32),
        ],
        scratch_shapes=[
            pltpu.VMEM((ring.size, width), bf16),
            pltpu.VMEM((ring.size, width), bf16),
            pltpu.VMEM((cells, width), f32),
            pltpu.VMEM(w_qkv.shape, bf16),
            pltpu.VMEM(w_out.shape, bf16),
            pltpu.VMEM((chunks, 2, block, CHUNK), bf16),
            pltpu.VMEM((chunks, 2, block, CHUNK), bf16),
            pltpu.VMEM((chunks, 2, groups, share, CHUNK), bf16),
            pltpu.VMEM((chunks, 2, groups, share, CHUNK), bf16),
            pltpu.VMEM((chunks, 2, groups, share, CHUNK), f32),
            pltpu.VMEM((chunks, groups, share, CHUNK), bf16),
            pltpu.VMEM((chunks, groups, share, CHUNK), bf16),
            pltpu.VMEM((chunks, groups, share, CHUNK), f32),
            pltpu.VMEM((chunks, groups - 1, share, CHUNK), bf16),
            pltpu.VMEM((chunks, groups - 1, share, CHUNK), bf16),
            pltpu.VMEM((chunks, share, CHUNK), f32),
            sems(2), sems(count), sems(count),
            sems(chunks), sems(chunks), sems(chunks), sems(chunks), sems(chunks), sems(chunks),
            sems(chunks, groups - 1), sems(chunks, groups - 1),
        ],
        compiler_params=pltpu.CompilerParams(
            collective_id=1, has_side_effects=True, vmem_limit_bytes=58 << 20
        ),
        cost_estimate=pl.CostEstimate(flops=14 << 30, bytes_accessed=20 << 20, transcendentals=cells),
    )(*operands)


def shards(tokens, norm_gain, w_qkv, w_out, cotangent):
    rows, cols, width = tokens.shape
    lats, lons = lax.axis_size("lat"), lax.axis_size("lon")
    scale = (rows * cols * lats * lons) ** (-0.5)
    ring = Ring(rows, cols)
    flat = tokens.reshape(-1, width)
    grad_flat = cotangent.reshape(-1, width)
    gain = norm_gain.reshape(1, width)
    query, grad_attended, keyval, normed_t = project(ring, lats, lons, flat, gain, grad_flat, w_qkv, w_out)
    attended, attended_t, grad_query, grad_key, grad_value = attention(ring, query, keyval, grad_attended)
    result, grad_tokens, grad_qkv, grad_out = finish(
        ring, lats, lons, scale,
        flat, gain, grad_flat, attended, attended_t, grad_query, grad_key, grad_value, normed_t, w_qkv, w_out,
    )
    return result.reshape(tokens.shape), grad_tokens.reshape(tokens.shape), grad_qkv, grad_out


def solution(mesh):
    placed = (P("lat", "lon", None), P(), P(), P(), P("lat", "lon", None))
    return jax.shard_map(
        shards,
        mesh=mesh,
        in_specs=placed,
        out_specs=(
            P("lat", "lon", None),
            P("lat", "lon", None),
            P(("lat", "lon"), None),
            P(("lat", "lon"), None),
        ),
        check_vma=False,
    )
```

```python
import functools

import jax
import jax.numpy as jnp
from jax import lax
from jax.experimental import pallas as pl
from jax.experimental.pallas import tpu as pltpu
from jax.sharding import PartitionSpec as P

H = 16
R = 6
SIDE = 8
PAIR = 128
TILE_ROWS = 8
CHUNK = 512
MESH = pl.DeviceIdType.MESH

epsilon = 1e-06
floor_score = -1e30

NT = (((1,), (1,)), ((), ()))
f32 = jnp.float32
bf16 = jnp.bfloat16


def dot(a, b, dims=(((1,), (0,)), ((), ()))):
    return lax.dot_general(a, b, dims, preferred_element_type=f32)


class Ring:
    def __init__(self, rows, cols):
        self.rows, self.cols = rows, cols
        self.row = R * cols
        self.corner = R * SIDE
        self.mid = rows * SIDE
        self.side = (rows + 2 * R) * SIDE
        self.west = 2 * self.row
        self.east = self.west + self.side
        self.size = self.east + self.side

    def pieces(self):
        found = [(-1, 0, 0, self.row), (1, 0, self.row, self.row)]
        for h, start in ((-1, self.west), (1, self.east)):
            found.append((-1, h, start, self.corner))
            found.append((0, h, start + self.corner, self.mid))
            found.append((1, h, start + self.corner + self.mid, self.corner))
        return found


def place_of(lats, lons):
    lat, lon = lax.axis_index("lat"), lax.axis_index("lon")
    return lat, lon, lat == 0, lat == lats - 1


def neighbour(lats, lons, v, h):
    lat, lon, north, south = place_of(lats, lons)
    polar = north if v < 0 else south
    if v == 0:
        return {"lat": lat, "lon": lax.rem(lon + h + lons, lons)}
    return {
        "lat": jnp.where(polar, lat, lat + v),
        "lon": lax.rem(lon + h + lons + jnp.where(polar, lons // 2, 0), lons),
    }


def ring_copies(ring, lats, lons, src, dst, send_sem, recv_sem):
    lat, lon, north, south = place_of(lats, lons)
    offsets = {(v, h): (i, at) for i, (v, h, at, length) in enumerate(ring.pieces())}
    copies = []
    for i, (v, h, at, length) in enumerate(ring.pieces()):
        slot, low = offsets[(-v, -h)]
        if v != 0:
            same_slot, same_low = offsets[(v, -h)]
            polar = north if v < 0 else south
            slot = jnp.where(polar, same_slot, slot)
            low = pl.multiple_of(jnp.where(polar, same_low, low), 16)
        copies.append(
            pltpu.make_async_remote_copy(
                src_ref=src.at[pl.ds(at, length)],
                dst_ref=dst.at[pl.ds(low, length)],
                send_sem=send_sem.at[i],
                recv_sem=recv_sem.at[slot],
                device_id=neighbour(lats, lons, v, h),
                device_id_type=MESH,
            )
        )
    return copies


def ring_arrivals(ring, lats, lons, dst, send_sem, recv_sem):
    found = []
    for i, (v, h, at, length) in enumerate(ring.pieces()):
        found.append(
            pltpu.make_async_remote_copy(
                src_ref=dst.at[pl.ds(at, length)],
                dst_ref=dst.at[pl.ds(at, length)],
                send_sem=send_sem.at[i],
                recv_sem=recv_sem.at[i],
                device_id=neighbour(lats, lons, v, h),
                device_id_type=MESH,
            )
        )
    return found


def turned(cells, polar):
    flipped = jnp.concatenate([cells[r : r + 1] for r in reversed(range(R))], axis=0)
    return jnp.where(polar, flipped, cells)


def put(ref, at, cells):
    count = cells.shape[0] * cells.shape[1]
    ref[at : at + count, :] = cells.reshape(count, cells.shape[2]).astype(bf16)


def greet(devices):
    barrier = pltpu.get_barrier_semaphore()
    for device in devices:
        pl.semaphore_signal(barrier, inc=1, device_id=device, device_id_type=MESH)
    return barrier


class Sums:
    def __init__(self, lats, lons, width, count, columns):
        self.count, self.columns = count, columns
        self.groups = lons // 2
        self.share = width // (lats * lons)
        self.block = width // lats

    def scratch(self):
        n, c, g, s = self.count, self.columns, self.groups, self.share
        vmem = lambda shape, kind=bf16: pltpu.VMEM(shape, kind)
        sems = lambda *shape: pltpu.SemaphoreType.DMA(shape)
        return [
            vmem((n, 2, self.block, c)), vmem((n, 2, self.block, c)),
            vmem((n, 2, g, s, c)), vmem((n, 2, g, s, c)), vmem((n, 2, g, s, c), f32),
            vmem((n, g, s, c)), vmem((n, g, s, c)),
            vmem((n, g - 1, s, c)), vmem((n, g - 1, s, c)),
            sems(n), sems(n), sems(n), sems(n), sems(n), sems(n), sems(n, g - 1), sems(n, g - 1),
        ]

    def bind(self, refs, place, term):
        (self.send0, self.came0, self.send1, self.came1, self.keep, self.send2, self.came2,
         self.send3, self.came3, *self.sems) = refs
        self.place, self.term = place, term

    def remote(self, step, src, dst, index, device):
        send, recv = self.sems[2 * step], self.sems[2 * step + 1]
        return pltpu.make_async_remote_copy(
            src_ref=src.at[index], dst_ref=dst.at[index],
            send_sem=send.at[index], recv_sem=recv.at[index],
            device_id=device, device_id_type=MESH,
        )

    def copy0(self, c):
        return self.remote(0, self.send0, self.came0, c, self.place.sibling)

    def copy1(self, c, lat_first):
        device = self.place.across_lat if lat_first else self.place.across_lon
        return self.remote(1, self.send1, self.came1, c, device)

    def copy2(self, c, lat_first):
        device = self.place.across_lon if lat_first else self.place.across_lat
        return self.remote(2, self.send2, self.came2, c, device)

    def copy3(self, c, k):
        return self.remote(3, self.send3, self.came3, (c, k), self.place.along[k])

    def step0(self, c):
        for half in range(2):
            self.send0[c, half] = self.term(half, 1 - self.place.lo, c).astype(bf16)
        self.copy0(c).start()

    def step1(self, c, lat_first):
        place = self.place
        self.copy0(c).wait_recv()

        def value(half):
            total = self.term(half, place.lo, c) + self.came0[c, half].astype(f32)
            return total.reshape(self.groups, 2, self.share, self.columns)

        if lat_first:
            sent = value(1 - place.hi)
            for second in range(2):
                self.send1[c, second] = sent[:, second].astype(bf16)
            self.copy1(c, lat_first).start()
            kept = value(place.hi)
            for second in range(2):
                self.keep[c, second] = kept[:, second]
        else:
            first = place.bit == 0
            for half in range(2):
                both = value(half)
                self.send1[c, half] = jnp.where(first, both[:, 1], both[:, 0]).astype(bf16)
                self.keep[c, half] = jnp.where(first, both[:, 0], both[:, 1])
            self.copy1(c, lat_first).start()

    def mine(self, lat_first):
        return self.place.bit if lat_first else self.place.hi

    def step2(self, c, lat_first):
        mine = self.mine(lat_first)
        self.copy1(c, lat_first).wait_recv()
        self.send2[c] = (self.keep[c, 1 - mine] + self.came1[c, 1 - mine].astype(f32)).astype(bf16)
        self.copy2(c, lat_first).start()
        self.keep[c, mine] = self.keep[c, mine] + self.came1[c, mine].astype(f32)

    def step3(self, c, lat_first):
        mine, group = self.mine(lat_first), self.place.group
        self.copy2(c, lat_first).wait_recv()
        for k in range(self.groups - 1):
            to = lax.rem(group + k + 1, self.groups)
            self.send3[c, k] = (self.keep[c, mine, to] + self.came2[c, to].astype(f32)).astype(bf16)
            self.copy3(c, k).start()
        self.keep[c, mine, group] = self.keep[c, mine, group] + self.came2[c, group].astype(f32)

    def step4(self, c, lat_first):
        total = self.keep[c, self.mine(lat_first), self.place.group]
        for k in range(self.groups - 1):
            self.copy3(c, k).wait_recv()
            total = total + self.came3[c, k].astype(f32)
        return total

    def drain(self, c, lat_first):
        self.copy0(c).wait_send()
        self.copy1(c, lat_first).wait_send()
        self.copy2(c, lat_first).wait_send()
        for k in range(self.groups - 1):
            self.copy3(c, k).wait_send()


class Place:
    def __init__(self, lats, lons):
        lat, lon = lax.axis_index("lat"), lax.axis_index("lon")
        groups = lons // 2
        self.hi, self.lo = lax.div(lat, 2), lax.rem(lat, 2)
        self.group, self.bit = lax.div(lon, 2), lax.rem(lon, 2)
        self.sibling = {"lat": 2 * self.hi + 1 - self.lo, "lon": lon}
        self.across_lat = {"lat": 2 * (1 - self.hi) + self.lo, "lon": lon}
        self.across_lon = {"lat": lat, "lon": 2 * self.group + 1 - self.bit}
        self.along = [
            {"lat": lat, "lon": 2 * lax.rem(self.group + k, groups) + self.bit} for k in range(1, groups)
        ]

    def partners(self):
        return [self.sibling, self.across_lat, self.across_lon] + self.along


class Window:
    def __init__(self, ring):
        self.ring = ring
        self.tiles = ring.rows // TILE_ROWS
        self.queries = TILE_ROWS * ring.cols
        self.reach = TILE_ROWS + 2 * R
        self.mid = self.reach * ring.cols
        self.side = self.reach * SIDE
        self.keys = self.mid + 2 * self.side

    def mask(self):
        cols = self.ring.cols
        key = lax.broadcasted_iota(jnp.int32, (self.keys, 2 * self.queries), 0)
        query = lax.broadcasted_iota(jnp.int32, (self.keys, 2 * self.queries), 1)
        query = lax.rem(query, self.queries)
        in_mid = key < self.mid
        in_west = key < self.mid + self.side
        side_key = key - jnp.where(in_west, self.mid, self.mid + self.side)
        row = jnp.where(in_mid, lax.div(key, cols), lax.div(side_key, SIDE))
        side_col = lax.rem(side_key, SIDE) + jnp.where(in_west, -SIDE, cols)
        col = jnp.where(in_mid, lax.rem(key, cols), side_col)
        row_gap = row - lax.div(query, cols)
        col_gap = col - lax.rem(query, cols)
        allowed = (row_gap >= 0) & (row_gap <= 2 * R) & (col_gap >= -R) & (col_gap <= R)
        return jnp.where(allowed, 0.0, floor_score)

    def spans(self, tile):
        ring = self.ring
        cells = ring.rows * ring.cols
        first = tile * TILE_ROWS - R
        low, high = max(first, 0), min(first + self.reach, ring.rows)
        found = [(low * ring.cols, (high - low) * ring.cols, (low - first) * ring.cols)]
        if first < 0:
            found.append((cells, -first * ring.cols, 0))
        if first + self.reach > ring.rows:
            count = (first + self.reach - ring.rows) * ring.cols
            found.append((cells + ring.row, count, self.mid - count))
        side_low = cells + ring.west + tile * TILE_ROWS * SIDE
        found.append((side_low, self.side, self.mid))
        found.append((side_low + ring.side, self.side, self.mid + self.side))
        return sorted(found, key=lambda span: span[2])

    def cuts(self):
        found = {0, self.ring.rows * self.ring.cols + self.ring.size}
        for tile in range(self.tiles):
            for at, n, to in self.spans(tile):
                found |= {at, at + n}
        found = sorted(found)
        return list(zip(found, found[1:]))


def attend(window, pair, width, mask_ref, q_ref, kv_ref, ga_ref, att_ref, att_t_ref, gq_ref, gk_ref, gv_ref):
    queries = window.queries
    head = PAIR // 2
    lanes = pl.ds(pl.multiple_of(pair * PAIR, PAIR), PAIR)
    value_lanes = pl.ds(pl.multiple_of(width + pair * PAIR, PAIR), PAIR)
    upper = lax.broadcasted_iota(jnp.int32, (2 * queries, PAIR), 0) < queries
    left = lax.broadcasted_iota(jnp.int32, (2 * queries, PAIR), 1) < head
    own = upper == left
    upper_t = lax.broadcasted_iota(jnp.int32, (PAIR, 2 * queries), 0) < head
    left_t = lax.broadcasted_iota(jnp.int32, (PAIR, 2 * queries), 1) < queries
    own_t = upper_t == left_t

    def paired(some):
        twice = jnp.concatenate([some, some], axis=0)
        return jnp.where(own, twice, 0.0)

    def unpaired(both):
        picked = jnp.where(own_t, both, 0.0)
        return picked[:, :queries] + picked[:, queries:]

    def gathered(at_lanes, tile):
        return jnp.concatenate([kv_ref[at : at + n, at_lanes] for at, n, to in window.spans(tile)], axis=0)

    dks, dvs = [], []
    for tile in range(window.tiles):
        own_rows = slice(tile * queries, (tile + 1) * queries)
        k = gathered(lanes, tile)
        v = gathered(value_lanes, tile)
        k_t = jnp.transpose(k)
        v_t = jnp.transpose(v)
        q32 = q_ref[own_rows, lanes].astype(f32) * (head ** (-0.5))
        do32 = ga_ref[own_rows, lanes].astype(f32)
        q_pair = paired(q32).astype(bf16)
        do_pair32 = paired(do32)
        do_pair = do_pair32.astype(bf16)
        scores = dot(k, q_pair, NT) + mask_ref[...]
        highest = jnp.max(scores, axis=0, keepdims=True)
        raised = jnp.exp(scores - highest)
        chances = raised * (1.0 / jnp.sum(raised, axis=0, keepdims=True))
        chances_low = chances.astype(bf16)
        attended_t = dot(v_t, chances_low).astype(bf16).astype(f32)
        delta = jnp.sum(attended_t * jnp.transpose(do_pair32), axis=0, keepdims=True)
        attended = unpaired(attended_t)
        att_t_ref[lanes, own_rows] = attended.astype(bf16)
        att_ref[own_rows, lanes] = jnp.transpose(attended).astype(bf16)
        grad_chances = dot(v, do_pair, NT)
        grad_scores = (chances * (grad_chances - delta)).astype(bf16)
        grad_query = jnp.transpose(unpaired(dot(k_t, grad_scores)))
        gq_ref[own_rows, lanes] = (grad_query * (head ** (-0.5))).astype(bf16)
        dks.append(dot(grad_scores, q_pair))
        dvs.append(dot(chances_low, do_pair))

    for ref, parts in ((gk_ref, dks), (gv_ref, dvs)):
        for low, high in window.cuts():
            summed = None
            for tile, part in enumerate(parts):
                for at, n, to in window.spans(tile):
                    if at <= low and high <= at + n:
                        piece = part[to + low - at : to + high - at]
                        summed = piece if summed is None else summed + piece
            ref[low:high, lanes] = summed.astype(bf16)


def block_kernel(
    ring, lats, lons, scale, qkv_sums, out_sums,
    tok_hbm, gain_hbm, cot_hbm, wqkv_hbm, wout_hbm,
    result_ref, gtok_ref, gqkv_ref, gout_ref,
    tok_ref, gain_ref, cot_ref, wqkv, wout,
    own, stage, halo, back, q_ref, ga_ref, kv_ref, nt_ref,
    att_ref, att_t_ref, gq_ref, gk_ref, gv_ref, mask_ref, spread,
    load_sem, halo_send, halo_recv, back_send, back_recv, *sum_refs,
):
    rows, cols = ring.rows, ring.cols
    cells, width = tok_ref.shape
    lat, lon, north, south = place_of(lats, lons)
    place = Place(lats, lons)
    around = [neighbour(lats, lons, v, h) for v, h, at, length in ring.pieces()]
    greeted = around + place.partners()
    barrier = greet(greeted)
    loads = [
        pltpu.make_async_copy(src, dst, load_sem.at[i])
        for i, (src, dst) in enumerate(
            ((tok_hbm, tok_ref), (gain_hbm, gain_ref), (cot_hbm, cot_ref), (wout_hbm, wout), (wqkv_hbm, wqkv))
        )
    ]
    for load in loads:
        load.start()
    block = width // lats

    def qkv_term(half, side, c):
        low = pl.multiple_of((2 * half + side) * block, block)
        lanes = pl.ds(pl.multiple_of(c * PAIR, PAIR), PAIR)
        query = dot(nt_ref[pl.ds(low, block), :cells], gq_ref[:, lanes])
        both = jnp.concatenate([gk_ref[:, lanes], gv_ref[:, lanes]], axis=1)
        return jnp.concatenate([query, dot(nt_ref[pl.ds(low, block), :], both)], axis=1)

    def out_term(half, side, c):
        low = pl.multiple_of((2 * half + side) * block, block)
        columns = out_sums.columns
        return dot(att_t_ref[pl.ds(low, block), :], cot_ref[:, c * columns : (c + 1) * columns])

    split = len(sum_refs) // 2
    qkv_sums.bind(sum_refs[:split], place, qkv_term)
    out_sums.bind(sum_refs[split:], place, out_term)

    loads[0].wait()
    loads[1].wait()
    source = tok_ref[...].astype(f32)
    inverse = lax.rsqrt(jnp.mean(source * source, axis=-1, keepdims=True) + epsilon)
    normed = source * inverse * gain_ref[...]
    own[...] = normed.astype(bf16)
    grid = normed.reshape(rows, cols, width)
    top, bottom = turned(grid[:R], north), turned(grid[rows - R :], south)
    put(stage, 0, top)
    put(stage, ring.row, bottom)
    for start, c in ((ring.west, 0), (ring.east, cols - SIDE)):
        put(stage, start, top[:, c : c + SIDE])
        put(stage, start + ring.corner, grid[:, c : c + SIDE])
        put(stage, start + ring.corner + ring.mid, bottom[:, c : c + SIDE])
    pl.semaphore_wait(barrier, len(greeted))
    copies = ring_copies(ring, lats, lons, stage, halo, halo_send, halo_recv)
    for copy in copies:
        copy.start()

    tile = CHUNK
    loads[2].wait()
    loads[3].wait()
    for j in range(width // tile):
        at = slice(j * tile, (j + 1) * tile)
        ga_ref[:, at] = dot(cot_ref[...], wout[at, :], NT).astype(bf16)
    loads[4].wait()
    for j in range(width // tile):
        at = slice(j * tile, (j + 1) * tile)
        q_ref[:, at] = dot(own[...], wqkv[:, at]).astype(bf16)

    def keyval(source_ref, low):
        count = source_ref.shape[0]

        def one(j, carry):
            into = pl.ds(pl.multiple_of(j * tile, tile), tile)
            at = pl.ds(pl.multiple_of(width + j * tile, tile), tile)
            kv_ref[low : low + count, into] = dot(source_ref[...], wqkv[:, at]).astype(bf16)
            return carry

        lax.fori_loop(0, 2 * width // tile, one, 0)

    keyval(own, 0)
    nt_ref[:, :cells] = jnp.transpose(own[...])
    window = Window(ring)
    mask_ref[...] = window.mask()
    for arrival in ring_arrivals(ring, lats, lons, halo, halo_send, halo_recv):
        arrival.wait_recv()
    keyval(halo, cells)
    nt_ref[:, cells:] = jnp.transpose(halo[...])
    for copy in copies:
        copy.wait_send()

    pairs = width // PAIR

    def attend_pair(pair):
        attend(
            window, pair, width, mask_ref, q_ref, kv_ref, ga_ref, att_ref, att_t_ref, gq_ref, gk_ref, gv_ref
        )
        qkv_sums.step0(pair)

    def two_pairs(j, carry):
        attend_pair(2 * j)

        @pl.when(j >= 1)
        def _():
            qkv_sums.step1(2 * j - 1, False)

        @pl.when(j >= 2)
        def _():
            qkv_sums.step2(2 * j - 3, False)

        @pl.when(j >= 3)
        def _():
            qkv_sums.step3(2 * j - 5, False)

        attend_pair(2 * j + 1)
        qkv_sums.step1(2 * j, True)

        @pl.when(j >= 1)
        def _():
            qkv_sums.step2(2 * j - 2, True)

        @pl.when(j >= 2)
        def _():
            qkv_sums.step3(2 * j - 4, True)

        return carry

    lax.fori_loop(0, pairs // 2, two_pairs, 0)

    outs = out_sums.count
    for c in range(outs):
        out_sums.step0(c)
    qkv_sums.step1(pairs - 1, False)

    def halo_back(j, carry):
        at = pl.ds(pl.multiple_of(j * tile, tile), tile)
        part = dot(gk_ref[cells:, :], wqkv[at, width : 2 * width], NT)
        part = part + dot(gv_ref[cells:, :], wqkv[at, 2 * width :], NT)
        top = turned(part[: ring.row].reshape(R, cols, tile), north)
        bottom = turned(part[ring.row : 2 * ring.row].reshape(R, cols, tile), south)
        stage[: ring.row, at] = top.reshape(ring.row, tile).astype(bf16)
        stage[ring.row : 2 * ring.row, at] = bottom.reshape(ring.row, tile).astype(bf16)
        for start in (ring.west, ring.east):
            end = start + ring.side
            low, high = start + ring.corner, end - ring.corner
            first = turned(part[start:low].reshape(R, SIDE, tile), north)
            last = turned(part[high:end].reshape(R, SIDE, tile), south)
            stage[start:low, at] = first.reshape(ring.corner, tile).astype(bf16)
            stage[low:high, at] = part[low:high].astype(bf16)
            stage[high:end, at] = last.reshape(ring.corner, tile).astype(bf16)
        return carry

    lax.fori_loop(0, width // tile, halo_back, 0)
    ring_sent = ring_copies(ring, lats, lons, stage, back, back_send, back_recv)
    for copy in ring_sent:
        copy.start()
    for c in range(outs):
        out_sums.step1(c, True)

    first_of = lambda c: c % 2 == 0
    qkv_sums.step2(pairs - 3, first_of(pairs - 3))
    qkv_sums.step3(pairs - 5, first_of(pairs - 5))
    qkv_sums.step2(pairs - 2, first_of(pairs - 2))

    def own_spread(j, carry):
        at = pl.ds(pl.multiple_of(j * tile, tile), tile)
        part = dot(gq_ref[...], wqkv[at, :width], NT)
        part = part + dot(gk_ref[:cells, :], wqkv[at, width : 2 * width], NT)
        spread[:, at] = part + dot(gv_ref[:cells, :], wqkv[at, 2 * width :], NT)
        return carry

    def own_result(j, carry):
        at = pl.ds(pl.multiple_of(j * tile, tile), tile)
        result_ref[:, at] = (dot(att_ref[...], wout[:, at]) + tok_ref[:, at].astype(f32)).astype(bf16)
        return carry

    lax.fori_loop(0, width // tile, own_spread, 0)
    qkv_sums.step3(pairs - 4, first_of(pairs - 4))
    qkv_sums.step2(pairs - 1, first_of(pairs - 1))
    lax.fori_loop(0, width // tile, own_result, 0)
    for c in range(outs):
        out_sums.step2(c, True)
    for c in range(pairs - 3, pairs):
        qkv_sums.step3(c, first_of(c))
    for c in range(outs):
        out_sums.step3(c, True)

    for arrival in ring_arrivals(ring, lats, lons, back, back_send, back_recv):
        arrival.wait_recv()
    piece = lambda at, n, m: back[at : at + n * m, :].astype(f32).reshape(n, m, width)
    both = lambda at, n: jnp.concatenate(
        [piece(ring.west + at, n, SIDE), piece(ring.east + at, n, SIDE)], axis=1
    )
    top = piece(0, R, cols) + both(0, R)
    bottom = piece(ring.row, R, cols) + both(ring.corner + ring.mid, R)
    grad = spread[...].reshape(rows, cols, width) + both(ring.corner, rows)
    grad = jnp.concatenate([grad[:R] + top, grad[R : rows - R], grad[rows - R :] + bottom], axis=0)
    scaled = gain_ref[...] * grad.reshape(cells, width)
    source = tok_ref[...].astype(f32)
    inverse = lax.rsqrt(jnp.mean(source * source, axis=-1, keepdims=True) + epsilon)
    shift = inverse**3 * jnp.mean(source * scaled, axis=-1, keepdims=True)
    gtok_ref[...] = (cot_ref[...].astype(f32) + inverse * scaled - source * shift).astype(bf16)

    for c in range(pairs):
        total = qkv_sums.step4(c, first_of(c)) * scale
        for kind in range(3):
            low = kind * width + c * PAIR
            gqkv_ref[:, low : low + PAIR] = total[:, kind * PAIR : (kind + 1) * PAIR]
    for c in range(outs):
        columns = out_sums.columns
        gout_ref[:, c * columns : (c + 1) * columns] = out_sums.step4(c, True) * scale
    for copy in ring_sent:
        copy.wait_send()
    for c in range(pairs):
        qkv_sums.drain(c, first_of(c))
    for c in range(outs):
        out_sums.drain(c, True)


def whole_block(ring, lats, lons, scale, tokens, gain, cotangent, w_qkv, w_out):
    cells, width = tokens.shape
    frame = cells + ring.size
    vmem = pl.BlockSpec(memory_space=pltpu.VMEM)
    anywhere = pl.BlockSpec(memory_space=pl.ANY)
    count = len(ring.pieces())
    share = width // (lats * lons)
    sems = lambda *shape: pltpu.SemaphoreType.DMA(shape)
    held = lambda *shape: pltpu.VMEM(shape, bf16)
    window = Window(ring)
    qkv_sums = Sums(lats, lons, width, width // PAIR, 3 * PAIR)
    out_sums = Sums(lats, lons, width, width // CHUNK, CHUNK)
    return pl.pallas_call(
        functools.partial(block_kernel, ring, lats, lons, scale, qkv_sums, out_sums),
        in_specs=[anywhere] * 5,
        out_specs=[vmem] * 4,
        out_shape=[
            jax.ShapeDtypeStruct((cells, width), bf16),
            jax.ShapeDtypeStruct((cells, width), bf16),
            jax.ShapeDtypeStruct((share, 3 * width), f32),
            jax.ShapeDtypeStruct((share, width), f32),
        ],
        scratch_shapes=[
            held(cells, width), pltpu.VMEM(gain.shape, f32), held(cells, width),
            held(*w_qkv.shape), held(*w_out.shape),
            held(cells, width), held(ring.size, width), held(ring.size, width), held(ring.size, width),
            held(cells, width), held(cells, width), held(frame, 2 * width), held(width, frame),
            held(cells, width), held(width, cells), held(cells, width), held(frame, width), held(frame, width),
            pltpu.VMEM((window.keys, 2 * window.queries), f32), pltpu.VMEM((cells, width), f32),
            sems(5), sems(count), sems(count), sems(count), sems(count),
        ] + qkv_sums.scratch() + out_sums.scratch(),
        compiler_params=pltpu.CompilerParams(
            collective_id=0, has_side_effects=True, vmem_limit_bytes=60 << 20
        ),
        cost_estimate=pl.CostEstimate(
            flops=30 << 30, bytes_accessed=16 << 20, transcendentals=cells * window.keys * H
        ),
    )(tokens, gain, cotangent, w_qkv, w_out)


def shards(tokens, norm_gain, w_qkv, w_out, cotangent):
    rows, cols, width = tokens.shape
    lats, lons = lax.axis_size("lat"), lax.axis_size("lon")
    scale = (rows * cols * lats * lons) ** (-0.5)
    ring = Ring(rows, cols)
    flat = tokens.reshape(-1, width)
    grad_flat = cotangent.reshape(-1, width)
    gain = norm_gain.reshape(1, width)
    result, grad_tokens, grad_qkv, grad_out = whole_block(
        ring, lats, lons, scale, flat, gain, grad_flat, w_qkv, w_out
    )
    return result.reshape(tokens.shape), grad_tokens.reshape(tokens.shape), grad_qkv, grad_out


def solution(mesh):
    placed = (P("lat", "lon", None), P(), P(), P(), P("lat", "lon", None))
    return jax.shard_map(
        shards,
        mesh=mesh,
        in_specs=placed,
        out_specs=(
            P("lat", "lon", None),
            P("lat", "lon", None),
            P(("lat", "lon"), None),
            P(("lat", "lon"), None),
        ),
        check_vma=False,
    )
```

```python
import functools

import jax
import jax.numpy as jnp
from jax import lax
from jax.experimental import pallas as pl
from jax.experimental.pallas import tpu as pltpu
from jax.sharding import PartitionSpec as P

H = 16
R = 6
PAIR = 128
TILE_ROWS = 8
BAND = 8
LANES = 128
CHUNK = 512
MESH = pl.DeviceIdType.MESH

epsilon = 1e-06
floor_score = -1e30

NT = (((1,), (1,)), ((), ()))
f32 = jnp.float32
bf16 = jnp.bfloat16


def dot(a, b, dims=(((1,), (0,)), ((), ()))):
    return lax.dot_general(a, b, dims, preferred_element_type=f32)


class Ring:
    def __init__(self, rows, cols):
        self.rows, self.cols = rows, cols
        self.row = R * cols
        self.block = R * BAND
        self.side = 4 * self.block
        self.west = 2 * self.row
        self.east = self.west + self.side
        self.size = self.east + self.side
        self.padded = -(-(rows * cols + self.size) // 128) * 128 - rows * cols


class Place:
    def __init__(self, lats, lons):
        lat, lon = lax.axis_index("lat"), lax.axis_index("lon")
        groups = lons // 2
        self.north, self.south = lat == 0, lat == lats - 1
        self.hi, self.lo = lax.div(lat, 2), lax.rem(lat, 2)
        self.group, self.bit = lax.div(lon, 2), lax.rem(lon, 2)
        self.sibling = {"lat": 2 * self.hi + 1 - self.lo, "lon": lon}
        self.across_lat = {"lat": 2 * (1 - self.hi) + self.lo, "lon": lon}
        self.across_lon = {"lat": lat, "lon": 2 * self.group + 1 - self.bit}
        self.along = [
            {"lat": lat, "lon": 2 * lax.rem(self.group + k, groups) + self.bit} for k in range(1, groups)
        ]

        def beside(v_lat, polar, h):
            turn = jnp.where(polar, lons // 2, 0)
            return {"lat": jnp.where(polar, lat, v_lat), "lon": lax.rem(lon + h + lons + turn, lons)}

        self.above = beside(lat - 1, self.north, 0)
        self.below = beside(lat + 1, self.south, 0)
        self.beside_west = {"lat": lat, "lon": lax.rem(lon - 1 + lons, lons)}
        self.beside_east = {"lat": lat, "lon": lax.rem(lon + 1, lons)}
        upper = self.lo == 0
        self.polar = self.north | self.south
        outer_lat = jnp.where(upper, lat - 1, lat + 1)
        self.outer_west = beside(outer_lat, self.polar, -1)
        self.outer_east = beside(outer_lat, self.polar, 1)

    def partners(self):
        return [
            self.above, self.below, self.beside_west, self.beside_east, self.outer_west, self.outer_east,
            self.sibling, self.across_lat, self.across_lon,
        ] + self.along


def remote(src, dst, send_sem, recv_sem, device):
    return pltpu.make_async_remote_copy(
        src_ref=src, dst_ref=dst, send_sem=send_sem, recv_sem=recv_sem,
        device_id=device, device_id_type=MESH,
    )


TOP, BOTTOM, WEST, EAST, OUTER_WEST, OUTER_EAST, INNER_WEST, INNER_EAST = range(8)


def strip_blocks(ref, first_col, cols, row):
    return jnp.concatenate(
        [
            jnp.concatenate(
                [ref[g, pl.ds(row * cols + first_col + c, BAND, stride=cols), :] for c in range(R)], axis=0
            )
            for g in range(ref.shape[0])
        ],
        axis=1,
    )


def put_lanes(ref, first, value):
    for g in range(value.shape[1] // LANES):
        ref[first + g] = value[:, g * LANES : (g + 1) * LANES]


def greet(devices):
    barrier = pltpu.get_barrier_semaphore()
    for device in devices:
        pl.semaphore_signal(barrier, inc=1, device_id=device, device_id_type=MESH)
    return barrier


def either(choice, first, second):
    if isinstance(choice, bool):
        return first if choice else second
    if isinstance(first, dict):
        return {name: jnp.where(choice, first[name], second[name]) for name in first}
    return jnp.where(choice, first, second)


def lat_first_of(chunk):
    return chunk % 3 != 0 if isinstance(chunk, int) else lax.rem(chunk, 3) != 0


class Sums:
    def __init__(self, lats, lons, width, count, columns):
        self.count, self.columns = count, columns
        self.groups = lons // 2
        self.share = width // (lats * lons)
        self.block = width // lats

    def scratch(self):
        n, c, g, s = self.count, self.columns, self.groups, self.share
        vmem = lambda shape, kind=bf16: pltpu.VMEM(shape, kind)
        sems = lambda *shape: pltpu.SemaphoreType.DMA(shape)
        return [
            vmem((n, 2, self.block, c)), vmem((n, 2, self.block, c)),
            vmem((n, 2, g, s, c)), vmem((n, 2, g, s, c)), vmem((n, 2, g, s, c), f32),
            vmem((n, g, s, c)), vmem((n, g, s, c)),
            vmem((n, g - 1, s, c)), vmem((n, g - 1, s, c)),
            sems(n), sems(n), sems(n), sems(n), sems(n), sems(n), sems(n, g - 1), sems(n, g - 1),
        ]

    def bind(self, refs, place, term):
        (self.send0, self.came0, self.send1, self.came1, self.keep, self.send2, self.came2,
         self.send3, self.came3, *self.sems) = refs
        self.place, self.term = place, term

    def remote(self, step, src, dst, index, device):
        send, recv = self.sems[2 * step], self.sems[2 * step + 1]
        return remote(src.at[index], dst.at[index], send.at[index], recv.at[index], device)

    def copy0(self, c):
        return self.remote(0, self.send0, self.came0, c, self.place.sibling)

    def copy1(self, c, lat_first):
        device = either(lat_first, self.place.across_lat, self.place.across_lon)
        return self.remote(1, self.send1, self.came1, c, device)

    def copy2(self, c, lat_first):
        device = either(lat_first, self.place.across_lon, self.place.across_lat)
        return self.remote(2, self.send2, self.came2, c, device)

    def copy3(self, c, k):
        return self.remote(3, self.send3, self.came3, (c, k), self.place.along[k])

    def step0(self, c):
        for half in range(2):
            self.send0[c, half] = self.term(half, 1 - self.place.lo, c).astype(bf16)
        self.copy0(c).start()

    def step1(self, c, lat_first):
        place = self.place
        self.copy0(c).wait_recv()

        def value(half):
            total = self.term(half, place.lo, c) + self.came0[c, half].astype(f32)
            return total.reshape(self.groups, 2, self.share, self.columns)

        def by_lat():
            sent = value(1 - place.hi)
            for second in range(2):
                self.send1[c, second] = sent[:, second].astype(bf16)
            self.copy1(c, True).start()
            kept = value(place.hi)
            for second in range(2):
                self.keep[c, second] = kept[:, second]

        def by_lon():
            first = place.bit == 0
            for half in range(2):
                both = value(half)
                self.send1[c, half] = jnp.where(first, both[:, 1], both[:, 0]).astype(bf16)
                self.keep[c, half] = jnp.where(first, both[:, 0], both[:, 1])
            self.copy1(c, False).start()

        if isinstance(lat_first, bool):
            by_lat() if lat_first else by_lon()
        else:
            pl.when(lat_first)(by_lat)
            pl.when(jnp.logical_not(lat_first))(by_lon)

    def mine(self, lat_first):
        return either(lat_first, self.place.bit, self.place.hi)

    def step2(self, c, lat_first):
        mine = self.mine(lat_first)
        self.copy1(c, lat_first).wait_recv()
        self.send2[c] = (self.keep[c, 1 - mine] + self.came1[c, 1 - mine].astype(f32)).astype(bf16)
        self.copy2(c, lat_first).start()
        self.keep[c, mine] = self.keep[c, mine] + self.came1[c, mine].astype(f32)

    def step3(self, c, lat_first):
        mine, group = self.mine(lat_first), self.place.group
        self.copy2(c, lat_first).wait_recv()
        for k in range(self.groups - 1):
            to = lax.rem(group + k + 1, self.groups)
            self.send3[c, k] = (self.keep[c, mine, to] + self.came2[c, to].astype(f32)).astype(bf16)
            self.copy3(c, k).start()
        self.keep[c, mine, group] = self.keep[c, mine, group] + self.came2[c, group].astype(f32)

    def step4(self, c, lat_first):
        total = self.keep[c, self.mine(lat_first), self.place.group]
        for k in range(self.groups - 1):
            self.copy3(c, k).wait_recv()
            total = total + self.came3[c, k].astype(f32)
        return total

    def drain(self, c, lat_first):
        self.copy0(c).wait_send()
        self.copy1(c, lat_first).wait_send()
        self.copy2(c, lat_first).wait_send()
        for k in range(self.groups - 1):
            self.copy3(c, k).wait_send()


class Window:
    def __init__(self, ring):
        self.ring = ring
        self.tiles = ring.rows // TILE_ROWS
        self.queries = TILE_ROWS * ring.cols
        self.reach = TILE_ROWS + 2 * R
        self.mid = self.reach * ring.cols
        self.side = 3 * ring.block
        self.keys = self.mid + 2 * self.side

    def mask(self, tile, north, south):
        rows, cols = self.ring.rows, self.ring.cols
        block = self.ring.block
        key = lax.broadcasted_iota(jnp.int32, (self.keys, 1), 0)
        query = lax.broadcasted_iota(jnp.int32, (1, 2 * self.queries), 1)
        query = lax.rem(query, self.queries)
        in_mid = key < self.mid
        in_west = key < self.mid + self.side
        side_key = key - jnp.where(in_west, self.mid, self.mid + self.side)
        side_row = (lax.div(side_key, block) + tile - 1) * BAND + lax.rem(side_key, BAND)
        side_col = lax.div(lax.rem(side_key, block), BAND) + jnp.where(in_west, -R, cols)
        row = jnp.where(in_mid, lax.div(key, cols) + tile * TILE_ROWS - R, side_row)
        col = jnp.where(in_mid, lax.rem(key, cols), side_col)
        deep = jnp.where(in_mid, R, BAND)
        row = jnp.where(north & (row < 0), -1 - (row + deep), row)
        row = jnp.where(south & (row >= rows), 2 * rows + deep - 1 - row, row)
        row_gap = row - (lax.div(query, cols) + tile * TILE_ROWS)
        col_gap = col - lax.rem(query, cols)
        allowed = (row_gap >= -R) & (row_gap <= R) & (col_gap >= -R) & (col_gap <= R)
        return jnp.where(allowed, 0.0, floor_score)

    def spans(self, tile):
        ring = self.ring
        cells = ring.rows * ring.cols
        first = tile * TILE_ROWS - R
        low, high = max(first, 0), min(first + self.reach, ring.rows)
        found = [(low * ring.cols, (high - low) * ring.cols, (low - first) * ring.cols)]
        if first < 0:
            found.append((cells, -first * ring.cols, 0))
        if first + self.reach > ring.rows:
            count = (first + self.reach - ring.rows) * ring.cols
            found.append((cells + ring.row, count, self.mid - count))
        side_low = cells + ring.west + tile * ring.block
        found.append((side_low, self.side, self.mid))
        found.append((side_low + ring.side, self.side, self.mid + self.side))
        return sorted(found, key=lambda span: span[2])

    def cuts(self):
        found = {0, self.ring.rows * self.ring.cols + self.ring.size}
        for tile in range(self.tiles):
            for at, n, to in self.spans(tile):
                found |= {at, at + n}
        found = sorted(found)
        return list(zip(found, found[1:]))


def attend(window, pair, width, mask_ref, q_ref, kv_ref, ga_ref, att_ref, att_t_ref, gq_ref, gk_ref, gv_ref):
    queries = window.queries
    head = PAIR // 2
    lanes = pl.ds(pl.multiple_of(pair * PAIR, PAIR), PAIR)
    value_lanes = pl.ds(pl.multiple_of(width + pair * PAIR, PAIR), PAIR)
    upper = lax.broadcasted_iota(jnp.int32, (2 * queries, PAIR), 0) < queries
    left = lax.broadcasted_iota(jnp.int32, (2 * queries, PAIR), 1) < head
    own = upper == left
    upper_t = lax.broadcasted_iota(jnp.int32, (PAIR, 2 * queries), 0) < head
    left_t = lax.broadcasted_iota(jnp.int32, (PAIR, 2 * queries), 1) < queries
    own_t = upper_t == left_t

    def paired(some):
        twice = jnp.concatenate([some, some], axis=0)
        return jnp.where(own, twice, 0.0)

    def unpaired(both):
        picked = jnp.where(own_t, both, 0.0)
        return picked[:, :queries] + picked[:, queries:]

    def gathered(at_lanes, tile):
        return jnp.concatenate([kv_ref[at : at + n, at_lanes] for at, n, to in window.spans(tile)], axis=0)

    dks, dvs = [], []
    for tile in range(window.tiles):
        own_rows = slice(tile * queries, (tile + 1) * queries)
        k = gathered(lanes, tile)
        v = gathered(value_lanes, tile)
        k_t = jnp.transpose(k)
        v_t = jnp.transpose(v)
        q32 = q_ref[own_rows, lanes].astype(f32) * (head ** (-0.5))
        do32 = ga_ref[own_rows, lanes].astype(f32)
        q_pair = paired(q32).astype(bf16)
        do_pair32 = paired(do32)
        do_pair = do_pair32.astype(bf16)
        scores = dot(k, q_pair, NT) + mask_ref[tile]
        highest = jnp.max(scores, axis=0, keepdims=True)
        raised = jnp.exp(scores - highest)
        chances = raised * (1.0 / jnp.sum(raised, axis=0, keepdims=True))
        chances_low = chances.astype(bf16)
        attended_t = dot(v_t, chances_low).astype(bf16).astype(f32)
        delta = jnp.sum(attended_t * jnp.transpose(do_pair32), axis=0, keepdims=True)
        attended = unpaired(attended_t)
        att_t_ref[lanes, own_rows] = attended.astype(bf16)
        att_ref[own_rows, lanes] = jnp.transpose(attended).astype(bf16)
        grad_chances = dot(v, do_pair, NT)
        grad_scores = (chances * (grad_chances - delta)).astype(bf16)
        grad_query = jnp.transpose(unpaired(dot(k_t, grad_scores)))
        gq_ref[own_rows, lanes] = (grad_query * (head ** (-0.5))).astype(bf16)
        dks.append(dot(grad_scores, q_pair))
        dvs.append(dot(chances_low, do_pair))

    for ref, parts in ((gk_ref, dks), (gv_ref, dvs)):
        for low, high in window.cuts():
            summed = None
            for tile, part in enumerate(parts):
                for at, n, to in window.spans(tile):
                    if at <= low and high <= at + n:
                        piece = part[to + low - at : to + high - at]
                        summed = piece if summed is None else summed + piece
            ref[low:high, lanes] = summed.astype(bf16)


def block_kernel(
    ring, lats, lons, scale, qkv_sums, out_sums,
    tok_hbm, gain_hbm, cot_hbm, wqkv_hbm, wout_hbm,
    result_ref, gtok_ref, gqkv_ref, gout_ref,
    tok_ref, gain_ref, cot_ref, wqkv, wout,
    own, strips, stage, halo, back, inner, q_ref, ga_ref, kv_ref, nt_ref,
    att_ref, att_t_ref, gq_ref, gk_ref, gv_ref, mask_ref, spread,
    load_sem, halo_send, halo_recv, back_send, back_recv, *sum_refs,
):
    rows, cols = ring.rows, ring.cols
    cells, width = tok_ref.shape
    place = Place(lats, lons)
    greeted = place.partners()
    barrier = greet(greeted)
    loads = [
        pltpu.make_async_copy(src, dst, load_sem.at[i])
        for i, (src, dst) in enumerate(
            ((tok_hbm, tok_ref), (gain_hbm, gain_ref), (cot_hbm, cot_ref), (wout_hbm, wout), (wqkv_hbm, wqkv))
        )
    ]
    for load in loads:
        load.start()
    block = width // lats

    def qkv_term(half, side, c):
        low = pl.multiple_of((2 * half + side) * block, block)
        lanes = pl.ds(pl.multiple_of(c * PAIR, PAIR), PAIR)
        query = dot(nt_ref[pl.ds(low, block), :cells], gq_ref[:, lanes])
        both = jnp.concatenate([gk_ref[:, lanes], gv_ref[:, lanes]], axis=1)
        return jnp.concatenate([query, dot(nt_ref[pl.ds(low, block), :], both)], axis=1)

    def out_term(half, side, c):
        low = pl.multiple_of((2 * half + side) * block, block)
        columns = out_sums.columns
        return dot(att_t_ref[pl.ds(low, block), :], cot_ref[:, c * columns : (c + 1) * columns])

    split = len(sum_refs) // 2
    qkv_sums.bind(sum_refs[:split], place, qkv_term)
    out_sums.bind(sum_refs[split:], place, out_term)

    loads[0].wait()
    loads[1].wait()
    source = tok_ref[...].astype(f32)
    inverse = lax.rsqrt(jnp.mean(source * source, axis=-1, keepdims=True) + epsilon)
    normed = source * inverse * gain_ref[...]
    own[...] = normed.astype(bf16)
    put_lanes(spread, 0, normed)
    half, block_cells = 2 * ring.block, ring.block
    for at, first_col in ((0, 0), (half, cols - R)):
        for band in range(2):
            low = at + band * block_cells
            strips[low : low + block_cells, :] = strip_blocks(spread, first_col, cols, band * BAND).astype(bf16)
    pl.semaphore_wait(barrier, len(greeted))

    upper = place.lo == 0
    rows16 = lambda at, count: pl.ds(pl.multiple_of(at, 16), count)
    to_above = jnp.where(place.north, TOP, BOTTOM)
    to_below = jnp.where(place.south, BOTTOM, TOP)
    at_above, at_below = to_above * ring.row, to_below * ring.row
    outer_there = jnp.where(upper == place.polar, 0, 3 * block_cells)
    outer_here = jnp.where(upper, 0, block_cells)
    halo_sems, back_sems = (halo_send, halo_recv), (back_send, back_recv)

    def send(src, src_at, dst, dst_at, count, sems, i, j, device):
        return remote(
            src.at[rows16(src_at, count)], dst.at[rows16(dst_at, count)], sems[0].at[i], sems[1].at[j], device
        )

    copies = [
        send(strips, 0, halo, ring.east + block_cells, half, halo_sems, WEST, EAST, place.beside_west),
        send(strips, half, halo, ring.west + block_cells, half, halo_sems, EAST, WEST, place.beside_east),
        send(strips, outer_here, halo, ring.east + outer_there, block_cells,
             halo_sems, OUTER_WEST, OUTER_EAST, place.outer_west),
        send(strips, half + outer_here, halo, ring.west + outer_there, block_cells,
             halo_sems, OUTER_EAST, OUTER_WEST, place.outer_east),
        send(own, 0, halo, at_above, ring.row, halo_sems, TOP, to_above, place.above),
        send(own, cells - ring.row, halo, at_below, ring.row, halo_sems, BOTTOM, to_below, place.below),
    ]
    for copy in copies:
        copy.start()
    halo[ring.size :, :] = jnp.zeros((ring.padded - ring.size, width), bf16)
    for ref in (gk_ref, gv_ref):
        ref[cells + ring.size :, :] = jnp.zeros((ring.padded - ring.size, width), bf16)

    tile = CHUNK
    loads[2].wait()
    loads[3].wait()
    for j in range(width // tile):
        at = slice(j * tile, (j + 1) * tile)
        ga_ref[:, at] = dot(cot_ref[...], wout[at, :], NT).astype(bf16)
    loads[4].wait()
    for j in range(width // tile):
        at = slice(j * tile, (j + 1) * tile)
        q_ref[:, at] = dot(own[...], wqkv[:, at]).astype(bf16)

    def keyval(source_ref, low):
        count = source_ref.shape[0]

        def one(j, carry):
            into = pl.ds(pl.multiple_of(j * tile, tile), tile)
            at = pl.ds(pl.multiple_of(width + j * tile, tile), tile)
            kv_ref[low : low + count, into] = dot(source_ref[...], wqkv[:, at]).astype(bf16)
            return carry

        lax.fori_loop(0, 2 * width // tile, one, 0)

    keyval(own, 0)
    nt_ref[:, :cells] = jnp.transpose(own[...])
    window = Window(ring)
    for t in range(window.tiles):
        mask_ref[t] = window.mask(t, place.north, place.south)

    inner_here = jnp.where(upper, 2 * block_cells, block_cells)
    inner_there = jnp.where(upper, 0, 3 * block_cells)

    def arrive(ref, at, count, sems, i):
        piece = ref.at[rows16(at, count)]
        remote(piece, piece, sems[0].at[i], sems[1].at[i], place.sibling).wait_recv()

    for i, j, start in ((WEST, INNER_WEST, ring.west), (EAST, INNER_EAST, ring.east)):
        arrive(halo, start + block_cells, half, halo_sems, i)
        copy = send(
            halo, start + inner_here, halo, start + inner_there, block_cells, halo_sems, j, j, place.sibling
        )
        copy.start()
        copies.append(copy)
    arrive(halo, 0, ring.row, halo_sems, TOP)
    arrive(halo, ring.row, ring.row, halo_sems, BOTTOM)
    outer_own = jnp.where(upper, 0, 3 * block_cells)
    inner_own = jnp.where(upper, 3 * block_cells, 0)
    for i, j, start in ((OUTER_WEST, INNER_WEST, ring.west), (OUTER_EAST, INNER_EAST, ring.east)):
        arrive(halo, start + outer_own, block_cells, halo_sems, i)
        arrive(halo, start + inner_own, block_cells, halo_sems, j)
    keyval(halo, cells)
    nt_ref[:, cells:] = jnp.transpose(halo[...])
    for copy in copies:
        copy.wait_send()

    pairs = width // PAIR

    def attend_pair(pair):
        attend(
            window, pair, width, mask_ref, q_ref, kv_ref, ga_ref, att_ref, att_t_ref, gq_ref, gk_ref, gv_ref
        )
        qkv_sums.step0(pair)

    def step(pair, carry):
        attend_pair(pair)

        @pl.when(pair >= 1)
        def _():
            qkv_sums.step1(pair - 1, lat_first_of(pair - 1))

        @pl.when(pair >= 3)
        def _():
            qkv_sums.step2(pair - 3, lat_first_of(pair - 3))

        @pl.when(pair >= 5)
        def _():
            qkv_sums.step3(pair - 5, lat_first_of(pair - 5))

        return carry

    lax.fori_loop(0, pairs, step, 0)

    outs = out_sums.count
    for c in range(outs):
        out_sums.step0(c)
    first_of = lat_first_of
    qkv_sums.step1(pairs - 1, first_of(pairs - 1))

    def halo_back(j, carry):
        at = pl.ds(pl.multiple_of(j * tile, tile), tile)
        some = slice(cells, cells + ring.size)
        part = dot(gk_ref[some, :], wqkv[at, width : 2 * width], NT)
        stage[:, at] = (part + dot(gv_ref[some, :], wqkv[at, 2 * width :], NT)).astype(bf16)
        return carry

    lax.fori_loop(0, width // tile, halo_back, 0)
    west_at, east_at = 2 * ring.row, 2 * ring.row + half
    outer_west_at, outer_east_at = east_at + half, east_at + half + block_cells
    inner_sent = [
        send(stage, ring.west + inner_own, inner, 0, block_cells, back_sems, INNER_WEST, INNER_WEST, place.sibling),
        send(stage, ring.east + inner_own, inner, block_cells, block_cells,
             back_sems, INNER_EAST, INNER_EAST, place.sibling),
    ]
    ring_sent = inner_sent + [
        send(stage, ring.west + outer_own, back, outer_east_at, block_cells,
             back_sems, OUTER_WEST, OUTER_EAST, place.outer_west),
        send(stage, ring.east + outer_own, back, outer_west_at, block_cells,
             back_sems, OUTER_EAST, OUTER_WEST, place.outer_east),
        send(stage, 0, back, at_above, ring.row, back_sems, TOP, to_above, place.above),
        send(stage, ring.row, back, at_below, ring.row, back_sems, BOTTOM, to_below, place.below),
    ]
    for copy in ring_sent:
        copy.start()
    out_sums.step1(0, True)
    for i, j, at, start, there, device in (
        (INNER_WEST, WEST, 0, ring.west, east_at, place.beside_west),
        (INNER_EAST, EAST, block_cells, ring.east, west_at, place.beside_east),
    ):
        arrive(inner, at, block_cells, back_sems, i)
        near = rows16(start + inner_here, block_cells)
        stage[near, :] = (
            stage[near, :].astype(f32) + inner[at : at + block_cells, :].astype(f32)
        ).astype(bf16)
        copy = send(
            stage, start + block_cells, back, there, half, back_sems, j, EAST if j == WEST else WEST, device
        )
        copy.start()
        ring_sent.append(copy)
    for c in range(1, outs):
        out_sums.step1(c, True)

    qkv_sums.step2(pairs - 3, first_of(pairs - 3))
    qkv_sums.step3(pairs - 5, first_of(pairs - 5))
    qkv_sums.step2(pairs - 2, first_of(pairs - 2))

    def own_spread(j, carry):
        at = pl.ds(pl.multiple_of(j * tile, tile), tile)
        part = dot(gq_ref[...], wqkv[at, :width], NT)
        part = part + dot(gk_ref[:cells, :], wqkv[at, width : 2 * width], NT)
        part = part + dot(gv_ref[:cells, :], wqkv[at, 2 * width :], NT)
        put_lanes(spread, j * (tile // LANES), part)
        return carry

    def own_result(j, carry):
        at = pl.ds(pl.multiple_of(j * tile, tile), tile)
        result_ref[:, at] = (dot(att_ref[...], wout[:, at]) + tok_ref[:, at].astype(f32)).astype(bf16)
        return carry

    lax.fori_loop(0, width // tile, own_spread, 0)
    qkv_sums.step3(pairs - 4, first_of(pairs - 4))
    qkv_sums.step2(pairs - 1, first_of(pairs - 1))
    lax.fori_loop(0, width // tile, own_result, 0)
    for c in range(outs):
        out_sums.step2(c, True)
    for c in range(pairs - 3, pairs):
        qkv_sums.step3(c, first_of(c))
    for c in range(outs):
        out_sums.step3(c, True)

    for i, at, count in (
        (TOP, 0, ring.row), (BOTTOM, ring.row, ring.row), (WEST, west_at, half), (EAST, east_at, half),
        (OUTER_WEST, outer_west_at, block_cells), (OUTER_EAST, outer_east_at, block_cells),
    ):
        arrive(back, at, count, back_sems, i)
    came = lambda at, count: back[at : at + count, :].astype(f32)
    groups = width // LANES
    lanes_of = lambda value, g: value[:, g * LANES : (g + 1) * LANES]
    for low, at in ((0, 0), (cells - ring.row, ring.row)):
        rows_back = came(at, ring.row)
        for g in range(groups):
            spread[g, low : low + ring.row, :] += lanes_of(rows_back, g)
    for at, outer_at, first_col in ((west_at, outer_west_at, 0), (east_at, outer_east_at, cols - R)):
        strip, outer = came(at, half), came(outer_at, block_cells)
        for band in range(2):
            here = jnp.where(place.lo == band, outer, 0.0)
            here = here + strip[band * block_cells : (band + 1) * block_cells]
            for c in range(R):
                line = pl.ds(band * BAND * cols + first_col + c, BAND, stride=cols)
                for g in range(groups):
                    spread[g, line, :] += lanes_of(here[c * BAND : (c + 1) * BAND], g)
    grad = jnp.concatenate([spread[g] for g in range(groups)], axis=1)
    scaled = gain_ref[...] * grad
    source = tok_ref[...].astype(f32)
    inverse = lax.rsqrt(jnp.mean(source * source, axis=-1, keepdims=True) + epsilon)
    shift = inverse**3 * jnp.mean(source * scaled, axis=-1, keepdims=True)
    gtok_ref[...] = (cot_ref[...].astype(f32) + inverse * scaled - source * shift).astype(bf16)

    for c in range(pairs):
        total = qkv_sums.step4(c, first_of(c)) * scale
        for kind in range(3):
            low = kind * width + c * PAIR
            gqkv_ref[:, low : low + PAIR] = total[:, kind * PAIR : (kind + 1) * PAIR]
    for c in range(outs):
        columns = out_sums.columns
        gout_ref[:, c * columns : (c + 1) * columns] = out_sums.step4(c, True) * scale
    for copy in ring_sent:
        copy.wait_send()
    for c in range(pairs):
        qkv_sums.drain(c, first_of(c))
    for c in range(outs):
        out_sums.drain(c, True)


def whole_block(ring, lats, lons, scale, tokens, gain, cotangent, w_qkv, w_out):
    cells, width = tokens.shape
    frame = cells + ring.padded
    vmem = pl.BlockSpec(memory_space=pltpu.VMEM)
    anywhere = pl.BlockSpec(memory_space=pl.ANY)
    count = 8
    share = width // (lats * lons)
    sems = lambda *shape: pltpu.SemaphoreType.DMA(shape)
    held = lambda *shape: pltpu.VMEM(shape, bf16)
    window = Window(ring)
    qkv_sums = Sums(lats, lons, width, width // PAIR, 3 * PAIR)
    out_sums = Sums(lats, lons, width, width // CHUNK, CHUNK)
    return pl.pallas_call(
        functools.partial(block_kernel, ring, lats, lons, scale, qkv_sums, out_sums),
        in_specs=[anywhere] * 5,
        out_specs=[vmem] * 4,
        out_shape=[
            jax.ShapeDtypeStruct((cells, width), bf16),
            jax.ShapeDtypeStruct((cells, width), bf16),
            jax.ShapeDtypeStruct((share, 3 * width), f32),
            jax.ShapeDtypeStruct((share, width), f32),
        ],
        scratch_shapes=[
            held(cells, width), pltpu.VMEM(gain.shape, f32), held(cells, width),
            held(*w_qkv.shape), held(*w_out.shape),
            held(cells, width), held(4 * ring.block, width), held(ring.size, width), held(ring.padded, width),
            held(ring.size, width), held(2 * ring.block, width),
            held(cells, width), held(cells, width), held(frame, 2 * width), held(width, frame),
            held(cells, width), held(width, cells), held(cells, width), held(frame, width), held(frame, width),
            pltpu.VMEM((window.tiles, window.keys, 2 * window.queries), f32), pltpu.VMEM((width // LANES, cells, LANES), f32),
            sems(5), sems(count), sems(count), sems(count), sems(count),
        ] + qkv_sums.scratch() + out_sums.scratch(),
        compiler_params=pltpu.CompilerParams(
            collective_id=0, has_side_effects=True, vmem_limit_bytes=60 << 20
        ),
        cost_estimate=pl.CostEstimate(
            flops=30 << 30, bytes_accessed=16 << 20, transcendentals=cells * window.keys * H
        ),
    )(tokens, gain, cotangent, w_qkv, w_out)


def shards(tokens, norm_gain, w_qkv, w_out, cotangent):
    rows, cols, width = tokens.shape
    lats, lons = lax.axis_size("lat"), lax.axis_size("lon")
    scale = (rows * cols * lats * lons) ** (-0.5)
    ring = Ring(rows, cols)
    flat = tokens.reshape(-1, width)
    grad_flat = cotangent.reshape(-1, width)
    gain = norm_gain.reshape(1, width)
    result, grad_tokens, grad_qkv, grad_out = whole_block(
        ring, lats, lons, scale, flat, gain, grad_flat, w_qkv, w_out
    )
    return result.reshape(tokens.shape), grad_tokens.reshape(tokens.shape), grad_qkv, grad_out


def solution(mesh):
    placed = (P("lat", "lon", None), P(), P(), P(), P("lat", "lon", None))
    return jax.shard_map(
        shards,
        mesh=mesh,
        in_specs=placed,
        out_specs=(
            P("lat", "lon", None),
            P("lat", "lon", None),
            P(("lat", "lon"), None),
            P(("lat", "lon"), None),
        ),
        check_vma=False,
    )
```

```python
import functools

import jax
import jax.numpy as jnp
from jax import lax
from jax.experimental import pallas as pl
from jax.experimental.pallas import tpu as pltpu
from jax.sharding import PartitionSpec as P

H = 16
R = 6
PAIR = 128
TILE_ROWS = 8
BAND = 8
LANES = 128
LAG2, LAG3 = 3, 5
LON_FIRST = (0, 2, 4, 6)
OUT_COLUMNS = 512
CHUNK = 512
MESH = pl.DeviceIdType.MESH

epsilon = 1e-06
floor_score = -1e30

NT = (((1,), (1,)), ((), ()))
f32 = jnp.float32
bf16 = jnp.bfloat16


def dot(a, b, dims=(((1,), (0,)), ((), ()))):
    return lax.dot_general(a, b, dims, preferred_element_type=f32)


class Ring:
    def __init__(self, rows, cols):
        self.rows, self.cols = rows, cols
        self.row = R * cols
        self.block = R * BAND
        self.side = 4 * self.block
        self.west = 2 * self.row
        self.east = self.west + self.side
        self.size = self.east + self.side
        self.padded = -(-(rows * cols + self.size) // 128) * 128 - rows * cols


class Place:
    def __init__(self, lats, lons):
        lat, lon = lax.axis_index("lat"), lax.axis_index("lon")
        groups = lons // 2
        self.north, self.south = lat == 0, lat == lats - 1
        self.hi, self.lo = lax.div(lat, 2), lax.rem(lat, 2)
        self.group, self.bit = lax.div(lon, 2), lax.rem(lon, 2)
        self.sibling = {"lat": 2 * self.hi + 1 - self.lo, "lon": lon}
        self.across_lat = {"lat": 2 * (1 - self.hi) + self.lo, "lon": lon}
        self.across_lon = {"lat": lat, "lon": 2 * self.group + 1 - self.bit}
        self.along = [
            {"lat": lat, "lon": 2 * lax.rem(self.group + k, groups) + self.bit} for k in range(1, groups)
        ]

        def beside(v_lat, polar, h):
            turn = jnp.where(polar, lons // 2, 0)
            return {"lat": jnp.where(polar, lat, v_lat), "lon": lax.rem(lon + h + lons + turn, lons)}

        self.above = beside(lat - 1, self.north, 0)
        self.below = beside(lat + 1, self.south, 0)
        self.beside_west = {"lat": lat, "lon": lax.rem(lon - 1 + lons, lons)}
        self.beside_east = {"lat": lat, "lon": lax.rem(lon + 1, lons)}
        upper = self.lo == 0
        self.polar = self.north | self.south
        outer_lat = jnp.where(upper, lat - 1, lat + 1)
        self.outer_west = beside(outer_lat, self.polar, -1)
        self.outer_east = beside(outer_lat, self.polar, 1)

    def partners(self):
        return [
            self.above, self.below, self.beside_west, self.beside_east, self.outer_west, self.outer_east,
            self.sibling, self.across_lat, self.across_lon,
        ] + self.along


def remote(src, dst, send_sem, recv_sem, device):
    return pltpu.make_async_remote_copy(
        src_ref=src, dst_ref=dst, send_sem=send_sem, recv_sem=recv_sem,
        device_id=device, device_id_type=MESH,
    )


TOP, BOTTOM, WEST, EAST, OUTER_WEST, OUTER_EAST, INNER_WEST, INNER_EAST = range(8)


def strip_blocks(ref, first_col, cols, row):
    return jnp.concatenate(
        [
            jnp.concatenate(
                [ref[g, pl.ds(row * cols + first_col + c, BAND, stride=cols), :] for c in range(R)], axis=0
            )
            for g in range(ref.shape[0])
        ],
        axis=1,
    )


def put_lanes(ref, first, value):
    for g in range(value.shape[1] // LANES):
        ref[first + g] = value[:, g * LANES : (g + 1) * LANES]


def greet(devices):
    barrier = pltpu.get_barrier_semaphore()
    for device in devices:
        pl.semaphore_signal(barrier, inc=1, device_id=device, device_id_type=MESH)
    return barrier


def either(choice, first, second):
    if isinstance(choice, bool):
        return first if choice else second
    if isinstance(first, dict):
        return {name: jnp.where(choice, first[name], second[name]) for name in first}
    return jnp.where(choice, first, second)


def lat_first_of(chunk):
    if isinstance(chunk, int):
        return chunk not in LON_FIRST
    first = chunk != LON_FIRST[0]
    for other in LON_FIRST[1:]:
        first = first & (chunk != other)
    return first


class Sums:
    def __init__(self, lats, lons, width, count, columns):
        self.count, self.columns = count, columns
        self.groups = lons // 2
        self.share = width // (lats * lons)
        self.block = width // lats

    def scratch(self):
        n, c, g, s = self.count, self.columns, self.groups, self.share
        vmem = lambda shape, kind=bf16: pltpu.VMEM(shape, kind)
        sems = lambda *shape: pltpu.SemaphoreType.DMA(shape)
        return [
            vmem((n, 2, self.block, c)), vmem((n, 2, self.block, c)),
            vmem((n, 2, g, s, c)), vmem((n, 2, g, s, c)), vmem((n, 2, g, s, c), f32),
            vmem((n, g, s, c)), vmem((n, g, s, c)),
            vmem((n, g - 1, s, c)), vmem((n, g - 1, s, c)),
            sems(n), sems(n), sems(n), sems(n), sems(n), sems(n), sems(n, g - 1), sems(n, g - 1),
        ]

    def bind(self, refs, place, term):
        (self.send0, self.came0, self.send1, self.came1, self.keep, self.send2, self.came2,
         self.send3, self.came3, *self.sems) = refs
        self.place, self.term = place, term

    def remote(self, step, src, dst, index, device):
        send, recv = self.sems[2 * step], self.sems[2 * step + 1]
        return remote(src.at[index], dst.at[index], send.at[index], recv.at[index], device)

    def copy0(self, c):
        return self.remote(0, self.send0, self.came0, c, self.place.sibling)

    def copy1(self, c, lat_first):
        device = either(lat_first, self.place.across_lat, self.place.across_lon)
        return self.remote(1, self.send1, self.came1, c, device)

    def copy2(self, c, lat_first):
        device = either(lat_first, self.place.across_lon, self.place.across_lat)
        return self.remote(2, self.send2, self.came2, c, device)

    def copy3(self, c, k):
        return self.remote(3, self.send3, self.came3, (c, k), self.place.along[k])

    def step0(self, c):
        for half in range(2):
            self.send0[c, half] = self.term(half, 1 - self.place.lo, c).astype(bf16)
        self.copy0(c).start()

    def step1(self, c, lat_first):
        place = self.place
        self.copy0(c).wait_recv()

        def value(half):
            total = self.term(half, place.lo, c) + self.came0[c, half].astype(f32)
            return total.reshape(self.groups, 2, self.share, self.columns)

        def by_lat():
            sent = value(1 - place.hi)
            for second in range(2):
                self.send1[c, second] = sent[:, second].astype(bf16)
            self.copy1(c, True).start()
            kept = value(place.hi)
            for second in range(2):
                self.keep[c, second] = kept[:, second]

        def by_lon():
            first = place.bit == 0
            for half in range(2):
                both = value(half)
                self.send1[c, half] = jnp.where(first, both[:, 1], both[:, 0]).astype(bf16)
                self.keep[c, half] = jnp.where(first, both[:, 0], both[:, 1])
            self.copy1(c, False).start()

        if isinstance(lat_first, bool):
            by_lat() if lat_first else by_lon()
        else:
            pl.when(lat_first)(by_lat)
            pl.when(jnp.logical_not(lat_first))(by_lon)

    def mine(self, lat_first):
        return either(lat_first, self.place.bit, self.place.hi)

    def step2(self, c, lat_first):
        mine = self.mine(lat_first)
        self.copy1(c, lat_first).wait_recv()
        self.send2[c] = (self.keep[c, 1 - mine] + self.came1[c, 1 - mine].astype(f32)).astype(bf16)
        self.copy2(c, lat_first).start()
        self.keep[c, mine] = self.keep[c, mine] + self.came1[c, mine].astype(f32)

    def step3(self, c, lat_first):
        mine, group = self.mine(lat_first), self.place.group
        self.copy2(c, lat_first).wait_recv()
        for k in range(self.groups - 1):
            to = lax.rem(group + k + 1, self.groups)
            self.send3[c, k] = (self.keep[c, mine, to] + self.came2[c, to].astype(f32)).astype(bf16)
            self.copy3(c, k).start()
        self.keep[c, mine, group] = self.keep[c, mine, group] + self.came2[c, group].astype(f32)

    def step4(self, c, lat_first):
        total = self.keep[c, self.mine(lat_first), self.place.group]
        for k in range(self.groups - 1):
            self.copy3(c, k).wait_recv()
            total = total + self.came3[c, k].astype(f32)
        return total

    def drain(self, c, lat_first):
        self.copy0(c).wait_send()
        self.copy1(c, lat_first).wait_send()
        self.copy2(c, lat_first).wait_send()
        for k in range(self.groups - 1):
            self.copy3(c, k).wait_send()


class Window:
    def __init__(self, ring):
        self.ring = ring
        self.tiles = ring.rows // TILE_ROWS
        self.queries = TILE_ROWS * ring.cols
        self.reach = TILE_ROWS + 2 * R
        self.mid = self.reach * ring.cols
        self.side = 3 * ring.block
        self.keys = self.mid + 2 * self.side

    def mask(self, tile, north, south):
        rows, cols = self.ring.rows, self.ring.cols
        block = self.ring.block
        key = lax.broadcasted_iota(jnp.int32, (self.keys, 1), 0)
        query = lax.broadcasted_iota(jnp.int32, (1, 2 * self.queries), 1)
        query = lax.rem(query, self.queries)
        in_mid = key < self.mid
        in_west = key < self.mid + self.side
        side_key = key - jnp.where(in_west, self.mid, self.mid + self.side)
        side_row = (lax.div(side_key, block) + tile - 1) * BAND + lax.rem(side_key, BAND)
        side_col = lax.div(lax.rem(side_key, block), BAND) + jnp.where(in_west, -R, cols)
        row = jnp.where(in_mid, lax.div(key, cols) + tile * TILE_ROWS - R, side_row)
        col = jnp.where(in_mid, lax.rem(key, cols), side_col)
        deep = jnp.where(in_mid, R, BAND)
        row = jnp.where(north & (row < 0), -1 - (row + deep), row)
        row = jnp.where(south & (row >= rows), 2 * rows + deep - 1 - row, row)
        row_gap = row - (lax.div(query, cols) + tile * TILE_ROWS)
        col_gap = col - lax.rem(query, cols)
        allowed = (row_gap >= -R) & (row_gap <= R) & (col_gap >= -R) & (col_gap <= R)
        return jnp.where(allowed, 0.0, floor_score)

    def spans(self, tile):
        ring = self.ring
        cells = ring.rows * ring.cols
        first = tile * TILE_ROWS - R
        low, high = max(first, 0), min(first + self.reach, ring.rows)
        found = [(low * ring.cols, (high - low) * ring.cols, (low - first) * ring.cols)]
        if first < 0:
            found.append((cells, -first * ring.cols, 0))
        if first + self.reach > ring.rows:
            count = (first + self.reach - ring.rows) * ring.cols
            found.append((cells + ring.row, count, self.mid - count))
        side_low = cells + ring.west + tile * ring.block
        found.append((side_low, self.side, self.mid))
        found.append((side_low + ring.side, self.side, self.mid + self.side))
        return sorted(found, key=lambda span: span[2])

    def cuts(self):
        found = {0, self.ring.rows * self.ring.cols + self.ring.size}
        for tile in range(self.tiles):
            for at, n, to in self.spans(tile):
                found |= {at, at + n}
        found = sorted(found)
        return list(zip(found, found[1:]))


def attend(window, pair, width, mask_ref, q_ref, kv_ref, ga_ref, att_ref, att_t_ref, gq_ref, gk_ref, gv_ref):
    queries = window.queries
    head = PAIR // 2
    lanes = pl.ds(pl.multiple_of(pair * PAIR, PAIR), PAIR)
    value_lanes = pl.ds(pl.multiple_of(width + pair * PAIR, PAIR), PAIR)
    upper = lax.broadcasted_iota(jnp.int32, (2 * queries, PAIR), 0) < queries
    left = lax.broadcasted_iota(jnp.int32, (2 * queries, PAIR), 1) < head
    own = upper == left
    upper_t = lax.broadcasted_iota(jnp.int32, (PAIR, 2 * queries), 0) < head
    left_t = lax.broadcasted_iota(jnp.int32, (PAIR, 2 * queries), 1) < queries
    own_t = upper_t == left_t

    def paired(some):
        twice = jnp.concatenate([some, some], axis=0)
        return jnp.where(own, twice, 0.0)

    def unpaired(both):
        picked = jnp.where(own_t, both, 0.0)
        return picked[:, :queries] + picked[:, queries:]

    def gathered(at_lanes, tile):
        return jnp.concatenate([kv_ref[at : at + n, at_lanes] for at, n, to in window.spans(tile)], axis=0)

    dks, dvs = [], []
    for tile in range(window.tiles):
        own_rows = slice(tile * queries, (tile + 1) * queries)
        k = gathered(lanes, tile)
        v = gathered(value_lanes, tile)
        k_t = jnp.transpose(k)
        v_t = jnp.transpose(v)
        q32 = q_ref[own_rows, lanes].astype(f32) * (head ** (-0.5))
        do32 = ga_ref[own_rows, lanes].astype(f32)
        q_pair = paired(q32).astype(bf16)
        do_pair32 = paired(do32)
        do_pair = do_pair32.astype(bf16)
        scores = dot(k, q_pair, NT) + mask_ref[tile]
        highest = jnp.max(scores, axis=0, keepdims=True)
        raised = jnp.exp(scores - highest)
        chances = raised * (1.0 / jnp.sum(raised, axis=0, keepdims=True))
        chances_low = chances.astype(bf16)
        attended_t = dot(v_t, chances_low).astype(bf16).astype(f32)
        delta = jnp.sum(attended_t * jnp.transpose(do_pair32), axis=0, keepdims=True)
        attended = unpaired(attended_t)
        att_t_ref[lanes, own_rows] = attended.astype(bf16)
        att_ref[own_rows, lanes] = jnp.transpose(attended).astype(bf16)
        grad_chances = dot(v, do_pair, NT)
        grad_scores = (chances * (grad_chances - delta)).astype(bf16)
        grad_query = jnp.transpose(unpaired(dot(k_t, grad_scores)))
        gq_ref[own_rows, lanes] = (grad_query * (head ** (-0.5))).astype(bf16)
        dks.append(dot(grad_scores, q_pair))
        dvs.append(dot(chances_low, do_pair))

    for ref, parts in ((gk_ref, dks), (gv_ref, dvs)):
        for low, high in window.cuts():
            summed = None
            for tile, part in enumerate(parts):
                for at, n, to in window.spans(tile):
                    if at <= low and high <= at + n:
                        piece = part[to + low - at : to + high - at]
                        summed = piece if summed is None else summed + piece
            ref[low:high, lanes] = summed.astype(bf16)


def block_kernel(
    ring, lats, lons, scale, qkv_sums, out_sums,
    tok_hbm, gain_hbm, cot_hbm, wqkv_hbm, wout_hbm,
    result_hbm, gtok_hbm, gqkv_hbm, gout_hbm,
    result_ref, gtok_ref, gqkv_ref, gout_ref,
    tok_ref, gain_ref, cot_ref, wqkv, wout,
    own, strips, stage, halo, back, inner, q_ref, ga_ref, kv_ref, nt_ref,
    att_ref, att_t_ref, gq_ref, gk_ref, gv_ref, mask_ref, spread,
    load_sem, store_sem, halo_send, halo_recv, back_send, back_recv, *sum_refs,
):
    rows, cols = ring.rows, ring.cols
    cells, width = tok_ref.shape
    place = Place(lats, lons)
    greeted = place.partners()
    barrier = greet(greeted)
    loads = [
        pltpu.make_async_copy(src, dst, load_sem.at[i])
        for i, (src, dst) in enumerate(
            ((tok_hbm, tok_ref), (gain_hbm, gain_ref), (cot_hbm, cot_ref), (wout_hbm, wout), (wqkv_hbm, wqkv))
        )
    ]
    for load in loads:
        load.start()
    stores = [
        pltpu.make_async_copy(src, dst, store_sem.at[i])
        for i, (src, dst) in enumerate(
            ((result_ref, result_hbm), (gtok_ref, gtok_hbm), (gqkv_ref, gqkv_hbm), (gout_ref, gout_hbm))
        )
    ]
    block = width // lats

    def qkv_term(half, side, c):
        low = pl.multiple_of((2 * half + side) * block, block)
        lanes = pl.ds(pl.multiple_of(c * PAIR, PAIR), PAIR)
        query = dot(nt_ref[pl.ds(low, block), :cells], gq_ref[:, lanes])
        both = jnp.concatenate([gk_ref[:, lanes], gv_ref[:, lanes]], axis=1)
        return jnp.concatenate([query, dot(nt_ref[pl.ds(low, block), :], both)], axis=1)

    def out_term(half, side, c):
        low = pl.multiple_of((2 * half + side) * block, block)
        columns = out_sums.columns
        return dot(att_t_ref[pl.ds(low, block), :], cot_ref[:, c * columns : (c + 1) * columns])

    split = len(sum_refs) // 2
    qkv_sums.bind(sum_refs[:split], place, qkv_term)
    out_sums.bind(sum_refs[split:], place, out_term)

    loads[0].wait()
    loads[1].wait()
    source = tok_ref[...].astype(f32)
    inverse = lax.rsqrt(jnp.mean(source * source, axis=-1, keepdims=True) + epsilon)
    normed = source * inverse * gain_ref[...]
    own[...] = normed.astype(bf16)
    put_lanes(spread, 0, normed)
    half, block_cells = 2 * ring.block, ring.block
    for at, first_col in ((0, 0), (half, cols - R)):
        for band in range(2):
            low = at + band * block_cells
            strips[low : low + block_cells, :] = strip_blocks(spread, first_col, cols, band * BAND).astype(bf16)
    pl.semaphore_wait(barrier, len(greeted))

    upper = place.lo == 0
    rows16 = lambda at, count: pl.ds(pl.multiple_of(at, 16), count)
    to_above = jnp.where(place.north, TOP, BOTTOM)
    to_below = jnp.where(place.south, BOTTOM, TOP)
    at_above, at_below = to_above * ring.row, to_below * ring.row
    outer_there = jnp.where(upper == place.polar, 0, 3 * block_cells)
    outer_here = jnp.where(upper, 0, block_cells)
    halo_sems, back_sems = (halo_send, halo_recv), (back_send, back_recv)

    def send(src, src_at, dst, dst_at, count, sems, i, j, device):
        return remote(
            src.at[rows16(src_at, count)], dst.at[rows16(dst_at, count)], sems[0].at[i], sems[1].at[j], device
        )

    copies = [
        send(strips, 0, halo, ring.east + block_cells, half, halo_sems, WEST, EAST, place.beside_west),
        send(strips, half, halo, ring.west + block_cells, half, halo_sems, EAST, WEST, place.beside_east),
        send(strips, outer_here, halo, ring.east + outer_there, block_cells,
             halo_sems, OUTER_WEST, OUTER_EAST, place.outer_west),
        send(strips, half + outer_here, halo, ring.west + outer_there, block_cells,
             halo_sems, OUTER_EAST, OUTER_WEST, place.outer_east),
        send(own, 0, halo, at_above, ring.row, halo_sems, TOP, to_above, place.above),
        send(own, cells - ring.row, halo, at_below, ring.row, halo_sems, BOTTOM, to_below, place.below),
    ]
    for copy in copies:
        copy.start()
    halo[ring.size :, :] = jnp.zeros((ring.padded - ring.size, width), bf16)
    for ref in (gk_ref, gv_ref):
        ref[cells + ring.size :, :] = jnp.zeros((ring.padded - ring.size, width), bf16)

    tile = CHUNK
    loads[2].wait()
    loads[3].wait()
    for j in range(width // tile):
        at = slice(j * tile, (j + 1) * tile)
        ga_ref[:, at] = dot(cot_ref[...], wout[at, :], NT).astype(bf16)
    loads[4].wait()
    for j in range(width // tile):
        at = slice(j * tile, (j + 1) * tile)
        q_ref[:, at] = dot(own[...], wqkv[:, at]).astype(bf16)

    def keyval(source_ref, low):
        count = source_ref.shape[0]

        def one(j, carry):
            into = pl.ds(pl.multiple_of(j * tile, tile), tile)
            at = pl.ds(pl.multiple_of(width + j * tile, tile), tile)
            kv_ref[low : low + count, into] = dot(source_ref[...], wqkv[:, at]).astype(bf16)
            return carry

        lax.fori_loop(0, 2 * width // tile, one, 0)

    keyval(own, 0)
    nt_ref[:, :cells] = jnp.transpose(own[...])
    window = Window(ring)
    for t in range(window.tiles):
        mask_ref[t] = window.mask(t, place.north, place.south)

    inner_here = jnp.where(upper, 2 * block_cells, block_cells)
    inner_there = jnp.where(upper, 0, 3 * block_cells)

    def arrive(ref, at, count, sems, i):
        piece = ref.at[rows16(at, count)]
        remote(piece, piece, sems[0].at[i], sems[1].at[i], place.sibling).wait_recv()

    for i, j, start in ((WEST, INNER_WEST, ring.west), (EAST, INNER_EAST, ring.east)):
        arrive(halo, start + block_cells, half, halo_sems, i)
        copy = send(
            halo, start + inner_here, halo, start + inner_there, block_cells, halo_sems, j, j, place.sibling
        )
        copy.start()
        copies.append(copy)
    arrive(halo, 0, ring.row, halo_sems, TOP)
    arrive(halo, ring.row, ring.row, halo_sems, BOTTOM)
    outer_own = jnp.where(upper, 0, 3 * block_cells)
    inner_own = jnp.where(upper, 3 * block_cells, 0)
    for i, j, start in ((OUTER_WEST, INNER_WEST, ring.west), (OUTER_EAST, INNER_EAST, ring.east)):
        arrive(halo, start + outer_own, block_cells, halo_sems, i)
        arrive(halo, start + inner_own, block_cells, halo_sems, j)
    keyval(halo, cells)
    nt_ref[:, cells:] = jnp.transpose(halo[...])
    for copy in copies:
        copy.wait_send()

    pairs = width // PAIR

    def attend_pair(pair):
        attend(
            window, pair, width, mask_ref, q_ref, kv_ref, ga_ref, att_ref, att_t_ref, gq_ref, gk_ref, gv_ref
        )
        qkv_sums.step0(pair)

    def step(pair, carry):
        attend_pair(pair)

        @pl.when(pair >= 1)
        def _():
            qkv_sums.step1(pair - 1, lat_first_of(pair - 1))

        @pl.when(pair >= LAG2)
        def _():
            qkv_sums.step2(pair - LAG2, lat_first_of(pair - LAG2))

        @pl.when(pair >= LAG3)
        def _():
            qkv_sums.step3(pair - LAG3, lat_first_of(pair - LAG3))

        return carry

    lax.fori_loop(0, pairs, step, 0)

    outs = out_sums.count
    first_of = lat_first_of
    left2, left3 = list(range(pairs - LAG2, pairs)), list(range(pairs - LAG3, pairs))

    def advance():
        if left2 and (not left3 or left3[0] >= left2[0] - (LAG3 - LAG2)):
            c = left2.pop(0)
            qkv_sums.step2(c, first_of(c))
        elif left3:
            c = left3.pop(0)
            qkv_sums.step3(c, first_of(c))

    qkv_sums.step1(pairs - 1, first_of(pairs - 1))

    def halo_back(j, carry):
        at = pl.ds(pl.multiple_of(j * tile, tile), tile)
        some = slice(cells, cells + ring.size)
        part = dot(gk_ref[some, :], wqkv[at, width : 2 * width], NT)
        stage[:, at] = (part + dot(gv_ref[some, :], wqkv[at, 2 * width :], NT)).astype(bf16)
        return carry

    lax.fori_loop(0, width // tile, halo_back, 0)
    west_at, east_at = 2 * ring.row, 2 * ring.row + half
    outer_west_at, outer_east_at = east_at + half, east_at + half + block_cells
    inner_sent = [
        send(stage, ring.west + inner_own, inner, 0, block_cells, back_sems, INNER_WEST, INNER_WEST, place.sibling),
        send(stage, ring.east + inner_own, inner, block_cells, block_cells,
             back_sems, INNER_EAST, INNER_EAST, place.sibling),
    ]
    ring_sent = inner_sent + [
        send(stage, ring.west + outer_own, back, outer_east_at, block_cells,
             back_sems, OUTER_WEST, OUTER_EAST, place.outer_west),
        send(stage, ring.east + outer_own, back, outer_west_at, block_cells,
             back_sems, OUTER_EAST, OUTER_WEST, place.outer_east),
        send(stage, 0, back, at_above, ring.row, back_sems, TOP, to_above, place.above),
        send(stage, ring.row, back, at_below, ring.row, back_sems, BOTTOM, to_below, place.below),
    ]
    for copy in ring_sent:
        copy.start()
    for c in range(outs):
        out_sums.step0(c)
    for i, j, at, start, there, device in (
        (INNER_WEST, WEST, 0, ring.west, east_at, place.beside_west),
        (INNER_EAST, EAST, block_cells, ring.east, west_at, place.beside_east),
    ):
        arrive(inner, at, block_cells, back_sems, i)
        near = rows16(start + inner_here, block_cells)
        stage[near, :] = (
            stage[near, :].astype(f32) + inner[at : at + block_cells, :].astype(f32)
        ).astype(bf16)
        copy = send(
            stage, start + block_cells, back, there, half, back_sems, j, EAST if j == WEST else WEST, device
        )
        copy.start()
        ring_sent.append(copy)
    for c in range(outs):
        out_sums.step1(c, True)
    for c in range(4):
        advance()

    def own_spread(j, carry):
        at = pl.ds(pl.multiple_of(j * tile, tile), tile)
        part = dot(gq_ref[...], wqkv[at, :width], NT)
        part = part + dot(gk_ref[:cells, :], wqkv[at, width : 2 * width], NT)
        part = part + dot(gv_ref[:cells, :], wqkv[at, 2 * width :], NT)
        put_lanes(spread, j * (tile // LANES), part)
        return carry

    def own_result(j, carry):
        at = pl.ds(pl.multiple_of(j * tile, tile), tile)
        result_ref[:, at] = (dot(att_ref[...], wout[:, at]) + tok_ref[:, at].astype(f32)).astype(bf16)
        return carry

    lax.fori_loop(0, width // tile, own_spread, 0)
    advance()
    advance()
    lax.fori_loop(0, width // tile, own_result, 0)
    stores[0].start()
    while left2:
        advance()
    out_sums.step2(0, True)
    advance()
    for c in range(1, outs):
        out_sums.step2(c, True)
    while left3:
        advance()
    for c in range(outs):
        out_sums.step3(c, True)

    for i, at, count in (
        (TOP, 0, ring.row), (BOTTOM, ring.row, ring.row), (WEST, west_at, half), (EAST, east_at, half),
        (OUTER_WEST, outer_west_at, block_cells), (OUTER_EAST, outer_east_at, block_cells),
    ):
        arrive(back, at, count, back_sems, i)
    came = lambda at, count: back[at : at + count, :].astype(f32)
    groups = width // LANES
    lanes_of = lambda value, g: value[:, g * LANES : (g + 1) * LANES]
    for low, at in ((0, 0), (cells - ring.row, ring.row)):
        rows_back = came(at, ring.row)
        for g in range(groups):
            spread[g, low : low + ring.row, :] += lanes_of(rows_back, g)
    for at, outer_at, first_col in ((west_at, outer_west_at, 0), (east_at, outer_east_at, cols - R)):
        strip, outer = came(at, half), came(outer_at, block_cells)
        for band in range(2):
            here = jnp.where(place.lo == band, outer, 0.0)
            here = here + strip[band * block_cells : (band + 1) * block_cells]
            for c in range(R):
                line = pl.ds(band * BAND * cols + first_col + c, BAND, stride=cols)
                for g in range(groups):
                    spread[g, line, :] += lanes_of(here[c * BAND : (c + 1) * BAND], g)
    grad = jnp.concatenate([spread[g] for g in range(groups)], axis=1)
    scaled = gain_ref[...] * grad
    source = tok_ref[...].astype(f32)
    inverse = lax.rsqrt(jnp.mean(source * source, axis=-1, keepdims=True) + epsilon)
    shift = inverse**3 * jnp.mean(source * scaled, axis=-1, keepdims=True)
    gtok_ref[...] = (cot_ref[...].astype(f32) + inverse * scaled - source * shift).astype(bf16)
    stores[1].start()

    for c in range(pairs):
        total = qkv_sums.step4(c, first_of(c)) * scale
        for kind in range(3):
            low = kind * width + c * PAIR
            gqkv_ref[:, low : low + PAIR] = total[:, kind * PAIR : (kind + 1) * PAIR]
    stores[2].start()
    for c in range(outs):
        columns = out_sums.columns
        gout_ref[:, c * columns : (c + 1) * columns] = out_sums.step4(c, True) * scale
    stores[3].start()
    for copy in ring_sent:
        copy.wait_send()
    for c in range(pairs):
        qkv_sums.drain(c, first_of(c))
    for c in range(outs):
        out_sums.drain(c, True)
    for store in stores:
        store.wait()


def whole_block(ring, lats, lons, scale, tokens, gain, cotangent, w_qkv, w_out):
    cells, width = tokens.shape
    frame = cells + ring.padded
    anywhere = pl.BlockSpec(memory_space=pl.ANY)
    count = 8
    share = width // (lats * lons)
    sems = lambda *shape: pltpu.SemaphoreType.DMA(shape)
    held = lambda *shape: pltpu.VMEM(shape, bf16)
    window = Window(ring)
    qkv_sums = Sums(lats, lons, width, width // PAIR, 3 * PAIR)
    out_sums = Sums(lats, lons, width, width // OUT_COLUMNS, OUT_COLUMNS)
    return pl.pallas_call(
        functools.partial(block_kernel, ring, lats, lons, scale, qkv_sums, out_sums),
        in_specs=[anywhere] * 5,
        out_specs=[anywhere] * 4,
        out_shape=[
            jax.ShapeDtypeStruct((cells, width), bf16),
            jax.ShapeDtypeStruct((cells, width), bf16),
            jax.ShapeDtypeStruct((share, 3 * width), f32),
            jax.ShapeDtypeStruct((share, width), f32),
        ],
        scratch_shapes=[
            held(cells, width), held(cells, width),
            pltpu.VMEM((share, 3 * width), f32), pltpu.VMEM((share, width), f32),
            held(cells, width), pltpu.VMEM(gain.shape, f32), held(cells, width),
            held(*w_qkv.shape), held(*w_out.shape),
            held(cells, width), held(4 * ring.block, width), held(ring.size, width), held(ring.padded, width),
            held(ring.size, width), held(2 * ring.block, width),
            held(cells, width), held(cells, width), held(frame, 2 * width), held(width, frame),
            held(cells, width), held(width, cells), held(cells, width), held(frame, width), held(frame, width),
            pltpu.VMEM((window.tiles, window.keys, 2 * window.queries), f32), pltpu.VMEM((width // LANES, cells, LANES), f32),
            sems(5), sems(4), sems(count), sems(count), sems(count), sems(count),
        ] + qkv_sums.scratch() + out_sums.scratch(),
        compiler_params=pltpu.CompilerParams(
            collective_id=0, has_side_effects=True, vmem_limit_bytes=60 << 20
        ),
        cost_estimate=pl.CostEstimate(
            flops=30 << 30, bytes_accessed=16 << 20, transcendentals=cells * window.keys * H
        ),
    )(tokens, gain, cotangent, w_qkv, w_out)


def deliver(*arrays):
    count = len(arrays)

    def kernel(*refs):
        sources, targets, held = refs[:count], refs[count : 2 * count], refs[2 * count : 3 * count]
        sem_in, sem_out = refs[-2:]
        reads = [pltpu.make_async_copy(sources[i], held[i], sem_in.at[i]) for i in range(count)]
        writes = [pltpu.make_async_copy(held[i], targets[i], sem_out.at[i]) for i in range(count)]
        for read in reads:
            read.start()
        for read, write in zip(reads, writes):
            read.wait()
            write.start()
        for write in writes:
            write.wait()

    anywhere = pl.BlockSpec(memory_space=pl.ANY)
    return pl.pallas_call(
        kernel,
        in_specs=[anywhere] * count,
        out_specs=[anywhere] * count,
        out_shape=[jax.ShapeDtypeStruct(array.shape, array.dtype) for array in arrays],
        scratch_shapes=[pltpu.VMEM(array.shape, array.dtype) for array in arrays]
        + [pltpu.SemaphoreType.DMA((count,))] * 2,
        cost_estimate=pl.CostEstimate(flops=0, bytes_accessed=4 << 20, transcendentals=0),
    )(*arrays)


def shards(tokens, norm_gain, w_qkv, w_out, cotangent):
    rows, cols, width = tokens.shape
    lats, lons = lax.axis_size("lat"), lax.axis_size("lon")
    scale = (rows * cols * lats * lons) ** (-0.5)
    ring = Ring(rows, cols)
    flat = tokens.reshape(-1, width)
    grad_flat = cotangent.reshape(-1, width)
    gain = norm_gain.reshape(1, width)
    result, grad_tokens, grad_qkv, grad_out = deliver(
        *whole_block(ring, lats, lons, scale, flat, gain, grad_flat, w_qkv, w_out)
    )
    return result.reshape(tokens.shape), grad_tokens.reshape(tokens.shape), grad_qkv, grad_out


def solution(mesh):
    placed = (P("lat", "lon", None), P(), P(), P(), P("lat", "lon", None))
    return jax.shard_map(
        shards,
        mesh=mesh,
        in_specs=placed,
        out_specs=(
            P("lat", "lon", None),
            P("lat", "lon", None),
            P(("lat", "lon"), None),
            P(("lat", "lon"), None),
        ),
        check_vma=False,
    )
```

```python
import functools

import jax
import jax.numpy as jnp
from jax import lax
from jax.experimental import pallas as pl
from jax.experimental.pallas import tpu as pltpu
from jax.sharding import PartitionSpec as P

H = 16
R = 6
PAIR = 128
TILE_ROWS = 8
BAND = 8
LANES = 128
LAG2, LAG3 = 3, 5
LON_FIRST = (0, 2, 4, 6)
OUT_COLUMNS = 512
CHUNK = 512
MESH = pl.DeviceIdType.MESH

epsilon = 1e-06
floor_score = -1e30

NT = (((1,), (1,)), ((), ()))
f32 = jnp.float32
bf16 = jnp.bfloat16


def dot(a, b, dims=(((1,), (0,)), ((), ()))):
    return lax.dot_general(a, b, dims, preferred_element_type=f32)


class Ring:
    def __init__(self, rows, cols):
        self.rows, self.cols = rows, cols
        self.row = R * cols
        self.block = R * BAND
        self.side = 4 * self.block
        self.west = 2 * self.row
        self.east = self.west + self.side
        self.size = self.east + self.side
        self.padded = -(-(rows * cols + self.size) // 128) * 128 - rows * cols


class Place:
    def __init__(self, lats, lons):
        lat, lon = lax.axis_index("lat"), lax.axis_index("lon")
        groups = lons // 2
        self.north, self.south = lat == 0, lat == lats - 1
        self.hi, self.lo = lax.div(lat, 2), lax.rem(lat, 2)
        self.group, self.bit = lax.div(lon, 2), lax.rem(lon, 2)
        self.sibling = {"lat": 2 * self.hi + 1 - self.lo, "lon": lon}
        self.across_lat = {"lat": 2 * (1 - self.hi) + self.lo, "lon": lon}
        self.across_lon = {"lat": lat, "lon": 2 * self.group + 1 - self.bit}
        self.along = [
            {"lat": lat, "lon": 2 * lax.rem(self.group + k, groups) + self.bit} for k in range(1, groups)
        ]

        def beside(v_lat, polar, h):
            turn = jnp.where(polar, lons // 2, 0)
            return {"lat": jnp.where(polar, lat, v_lat), "lon": lax.rem(lon + h + lons + turn, lons)}

        self.above = beside(lat - 1, self.north, 0)
        self.below = beside(lat + 1, self.south, 0)
        self.beside_west = {"lat": lat, "lon": lax.rem(lon - 1 + lons, lons)}
        self.beside_east = {"lat": lat, "lon": lax.rem(lon + 1, lons)}
        upper = self.lo == 0
        self.polar = self.north | self.south
        outer_lat = jnp.where(upper, lat - 1, lat + 1)
        self.outer = {name: jnp.where(upper, self.above[name], self.below[name]) for name in ("lat", "lon")}
        self.outer_west = beside(outer_lat, self.polar, -1)
        self.outer_east = beside(outer_lat, self.polar, 1)

    def partners(self):
        return [
            self.above, self.below, self.beside_west, self.beside_east, self.outer_west, self.outer_east,
            self.sibling, self.across_lat, self.across_lon,
        ] + self.along


def remote(src, dst, send_sem, recv_sem, device):
    return pltpu.make_async_remote_copy(
        src_ref=src, dst_ref=dst, send_sem=send_sem, recv_sem=recv_sem,
        device_id=device, device_id_type=MESH,
    )


TOP, BOTTOM, WEST, EAST, OUTER_WEST, OUTER_EAST, INNER_WEST, INNER_EAST = range(8)
WEST_LATE, EAST_LATE = 8, 9


def strip_blocks(ref, first_col, cols, row):
    return jnp.concatenate(
        [
            jnp.concatenate(
                [ref[g, pl.ds(row * cols + first_col + c, BAND, stride=cols), :] for c in range(R)], axis=0
            )
            for g in range(ref.shape[0])
        ],
        axis=1,
    )


def put_lanes(ref, first, value):
    for g in range(value.shape[1] // LANES):
        ref[first + g] = value[:, g * LANES : (g + 1) * LANES]


def greet(devices):
    barrier = pltpu.get_barrier_semaphore()
    for device in devices:
        pl.semaphore_signal(barrier, inc=1, device_id=device, device_id_type=MESH)
    return barrier


def either(choice, first, second):
    if isinstance(choice, bool):
        return first if choice else second
    if isinstance(first, dict):
        return {name: jnp.where(choice, first[name], second[name]) for name in first}
    return jnp.where(choice, first, second)


def lat_first_of(chunk):
    if isinstance(chunk, int):
        return chunk not in LON_FIRST
    first = chunk != LON_FIRST[0]
    for other in LON_FIRST[1:]:
        first = first & (chunk != other)
    return first


class Sums:
    def __init__(self, lats, lons, width, count, columns):
        self.count, self.columns = count, columns
        self.groups = lons // 2
        self.share = width // (lats * lons)
        self.block = width // lats

    def scratch(self):
        n, c, g, s = self.count, self.columns, self.groups, self.share
        vmem = lambda shape, kind=bf16: pltpu.VMEM(shape, kind)
        sems = lambda *shape: pltpu.SemaphoreType.DMA(shape)
        return [
            vmem((n, 2, self.block, c)), vmem((n, 2, self.block, c)),
            vmem((n, 2, g, s, c)), vmem((n, 2, g, s, c)), vmem((n, 2, g, s, c), f32),
            vmem((n, g, s, c)), vmem((n, g, s, c)),
            vmem((n, g - 1, s, c)), vmem((n, g - 1, s, c)),
            sems(n), sems(n), sems(n), sems(n), sems(n), sems(n), sems(n, g - 1), sems(n, g - 1),
        ]

    def bind(self, refs, place, term):
        (self.send0, self.came0, self.send1, self.came1, self.keep, self.send2, self.came2,
         self.send3, self.came3, *self.sems) = refs
        self.place, self.term = place, term

    def remote(self, step, src, dst, index, device):
        send, recv = self.sems[2 * step], self.sems[2 * step + 1]
        return remote(src.at[index], dst.at[index], send.at[index], recv.at[index], device)

    def copy0(self, c):
        return self.remote(0, self.send0, self.came0, c, self.place.sibling)

    def copy1(self, c, lat_first):
        device = either(lat_first, self.place.across_lat, self.place.across_lon)
        return self.remote(1, self.send1, self.came1, c, device)

    def copy2(self, c, lat_first):
        device = either(lat_first, self.place.across_lon, self.place.across_lat)
        return self.remote(2, self.send2, self.came2, c, device)

    def copy3(self, c, k):
        return self.remote(3, self.send3, self.came3, (c, k), self.place.along[k])

    def step0(self, c):
        for half in range(2):
            self.send0[c, half] = self.term(half, 1 - self.place.lo, c).astype(bf16)
        self.copy0(c).start()

    def step1(self, c, lat_first):
        place = self.place
        self.copy0(c).wait_recv()

        def value(half):
            total = self.term(half, place.lo, c) + self.came0[c, half].astype(f32)
            return total.reshape(self.groups, 2, self.share, self.columns)

        def by_lat():
            sent = value(1 - place.hi)
            for second in range(2):
                self.send1[c, second] = sent[:, second].astype(bf16)
            self.copy1(c, True).start()
            kept = value(place.hi)
            for second in range(2):
                self.keep[c, second] = kept[:, second]

        def by_lon():
            first = place.bit == 0
            for half in range(2):
                both = value(half)
                self.send1[c, half] = jnp.where(first, both[:, 1], both[:, 0]).astype(bf16)
                self.keep[c, half] = jnp.where(first, both[:, 0], both[:, 1])
            self.copy1(c, False).start()

        if isinstance(lat_first, bool):
            by_lat() if lat_first else by_lon()
        else:
            pl.when(lat_first)(by_lat)
            pl.when(jnp.logical_not(lat_first))(by_lon)

    def mine(self, lat_first):
        return either(lat_first, self.place.bit, self.place.hi)

    def step2(self, c, lat_first):
        mine = self.mine(lat_first)
        self.copy1(c, lat_first).wait_recv()
        self.send2[c] = (self.keep[c, 1 - mine] + self.came1[c, 1 - mine].astype(f32)).astype(bf16)
        self.copy2(c, lat_first).start()
        self.keep[c, mine] = self.keep[c, mine] + self.came1[c, mine].astype(f32)

    def step3(self, c, lat_first):
        mine, group = self.mine(lat_first), self.place.group
        self.copy2(c, lat_first).wait_recv()
        for k in range(self.groups - 1):
            to = lax.rem(group + k + 1, self.groups)
            self.send3[c, k] = (self.keep[c, mine, to] + self.came2[c, to].astype(f32)).astype(bf16)
            self.copy3(c, k).start()
        self.keep[c, mine, group] = self.keep[c, mine, group] + self.came2[c, group].astype(f32)

    def step4(self, c, lat_first):
        total = self.keep[c, self.mine(lat_first), self.place.group]
        for k in range(self.groups - 1):
            self.copy3(c, k).wait_recv()
            total = total + self.came3[c, k].astype(f32)
        return total

    def drain(self, c, lat_first):
        self.copy0(c).wait_send()
        self.copy1(c, lat_first).wait_send()
        self.copy2(c, lat_first).wait_send()
        for k in range(self.groups - 1):
            self.copy3(c, k).wait_send()


class Window:
    def __init__(self, ring):
        self.ring = ring
        self.tiles = ring.rows // TILE_ROWS
        self.queries = TILE_ROWS * ring.cols
        self.reach = TILE_ROWS + 2 * R
        self.mid = self.reach * ring.cols
        self.side = 3 * ring.block
        self.keys = self.mid + 2 * self.side

    def mask(self, tile, north, south):
        rows, cols = self.ring.rows, self.ring.cols
        block = self.ring.block
        key = lax.broadcasted_iota(jnp.int32, (self.keys, 1), 0)
        query = lax.broadcasted_iota(jnp.int32, (1, 2 * self.queries), 1)
        query = lax.rem(query, self.queries)
        in_mid = key < self.mid
        in_west = key < self.mid + self.side
        side_key = key - jnp.where(in_west, self.mid, self.mid + self.side)
        side_row = (lax.div(side_key, block) + tile - 1) * BAND + lax.rem(side_key, BAND)
        side_col = lax.div(lax.rem(side_key, block), BAND) + jnp.where(in_west, -R, cols)
        row = jnp.where(in_mid, lax.div(key, cols) + tile * TILE_ROWS - R, side_row)
        col = jnp.where(in_mid, lax.rem(key, cols), side_col)
        deep = jnp.where(in_mid, R, BAND)
        row = jnp.where(north & (row < 0), -1 - (row + deep), row)
        row = jnp.where(south & (row >= rows), 2 * rows + deep - 1 - row, row)
        row_gap = row - (lax.div(query, cols) + tile * TILE_ROWS)
        col_gap = col - lax.rem(query, cols)
        allowed = (row_gap >= -R) & (row_gap <= R) & (col_gap >= -R) & (col_gap <= R)
        return jnp.where(allowed, 0.0, floor_score)

    def spans(self, tile):
        ring = self.ring
        cells = ring.rows * ring.cols
        first = tile * TILE_ROWS - R
        low, high = max(first, 0), min(first + self.reach, ring.rows)
        found = [(low * ring.cols, (high - low) * ring.cols, (low - first) * ring.cols)]
        if first < 0:
            found.append((cells, -first * ring.cols, 0))
        if first + self.reach > ring.rows:
            count = (first + self.reach - ring.rows) * ring.cols
            found.append((cells + ring.row, count, self.mid - count))
        side_low = cells + ring.west + tile * ring.block
        found.append((side_low, self.side, self.mid))
        found.append((side_low + ring.side, self.side, self.mid + self.side))
        return sorted(found, key=lambda span: span[2])

    def cuts(self):
        found = {0, self.ring.rows * self.ring.cols + self.ring.size}
        for tile in range(self.tiles):
            for at, n, to in self.spans(tile):
                found |= {at, at + n}
        found = sorted(found)
        return list(zip(found, found[1:]))


def attend(window, pair, width, mask_ref, q_ref, kv_ref, ga_ref, att_ref, att_t_ref, gq_ref, gk_ref, gv_ref):
    queries = window.queries
    head = PAIR // 2
    lanes = pl.ds(pl.multiple_of(pair * PAIR, PAIR), PAIR)
    value_lanes = pl.ds(pl.multiple_of(width + pair * PAIR, PAIR), PAIR)
    upper = lax.broadcasted_iota(jnp.int32, (2 * queries, PAIR), 0) < queries
    left = lax.broadcasted_iota(jnp.int32, (2 * queries, PAIR), 1) < head
    own = upper == left
    upper_t = lax.broadcasted_iota(jnp.int32, (PAIR, 2 * queries), 0) < head
    left_t = lax.broadcasted_iota(jnp.int32, (PAIR, 2 * queries), 1) < queries
    own_t = upper_t == left_t

    def paired(some):
        twice = jnp.concatenate([some, some], axis=0)
        return jnp.where(own, twice, 0.0)

    def unpaired(both):
        picked = jnp.where(own_t, both, 0.0)
        return picked[:, :queries] + picked[:, queries:]

    def gathered(at_lanes, tile):
        return jnp.concatenate([kv_ref[at : at + n, at_lanes] for at, n, to in window.spans(tile)], axis=0)

    dks, dvs = [], []
    for tile in range(window.tiles):
        own_rows = slice(tile * queries, (tile + 1) * queries)
        k = gathered(lanes, tile)
        v = gathered(value_lanes, tile)
        k_t = jnp.transpose(k)
        v_t = jnp.transpose(v)
        q32 = q_ref[own_rows, lanes].astype(f32) * (head ** (-0.5))
        do32 = ga_ref[own_rows, lanes].astype(f32)
        q_pair = paired(q32).astype(bf16)
        do_pair32 = paired(do32)
        do_pair = do_pair32.astype(bf16)
        scores = dot(k, q_pair, NT) + mask_ref[tile]
        highest = jnp.max(scores, axis=0, keepdims=True)
        raised = jnp.exp(scores - highest)
        chances = raised * (1.0 / jnp.sum(raised, axis=0, keepdims=True))
        chances_low = chances.astype(bf16)
        attended_t = dot(v_t, chances_low).astype(bf16).astype(f32)
        delta = jnp.sum(attended_t * jnp.transpose(do_pair32), axis=0, keepdims=True)
        attended = unpaired(attended_t)
        att_t_ref[lanes, own_rows] = attended.astype(bf16)
        att_ref[own_rows, lanes] = jnp.transpose(attended).astype(bf16)
        grad_chances = dot(v, do_pair, NT)
        grad_scores = (chances * (grad_chances - delta)).astype(bf16)
        grad_query = jnp.transpose(unpaired(dot(k_t, grad_scores)))
        gq_ref[own_rows, lanes] = (grad_query * (head ** (-0.5))).astype(bf16)
        dks.append(dot(grad_scores, q_pair))
        dvs.append(dot(chances_low, do_pair))

    for ref, parts in ((gk_ref, dks), (gv_ref, dvs)):
        for low, high in window.cuts():
            summed = None
            for tile, part in enumerate(parts):
                for at, n, to in window.spans(tile):
                    if at <= low and high <= at + n:
                        piece = part[to + low - at : to + high - at]
                        summed = piece if summed is None else summed + piece
            ref[low:high, lanes] = summed.astype(bf16)


def block_kernel(
    ring, lats, lons, scale, qkv_sums, out_sums,
    tok_hbm, gain_hbm, cot_hbm, wqkv_hbm, wout_hbm,
    result_hbm, gtok_hbm, gqkv_hbm, gout_hbm,
    result_ref, gtok_ref, gqkv_ref, gout_ref,
    tok_ref, gain_ref, cot_ref, wqkv, wout,
    own, strips, stage, halo, back, inner, q_ref, ga_ref, kv_ref, nt_ref,
    att_ref, att_t_ref, gq_ref, gk_ref, gv_ref, mask_ref, spread,
    load_sem, store_sem, halo_send, halo_recv, back_send, back_recv, *sum_refs,
):
    rows, cols = ring.rows, ring.cols
    cells, width = tok_ref.shape
    place = Place(lats, lons)
    greeted = place.partners()
    barrier = greet(greeted)
    loads = [
        pltpu.make_async_copy(src, dst, load_sem.at[i])
        for i, (src, dst) in enumerate(
            ((tok_hbm, tok_ref), (gain_hbm, gain_ref), (cot_hbm, cot_ref), (wout_hbm, wout), (wqkv_hbm, wqkv))
        )
    ]
    for load in loads:
        load.start()
    stores = [
        pltpu.make_async_copy(src, dst, store_sem.at[i])
        for i, (src, dst) in enumerate(
            ((result_ref, result_hbm), (gtok_ref, gtok_hbm), (gqkv_ref, gqkv_hbm), (gout_ref, gout_hbm))
        )
    ]
    block = width // lats

    def qkv_term(half, side, c):
        low = pl.multiple_of((2 * half + side) * block, block)
        lanes = pl.ds(pl.multiple_of(c * PAIR, PAIR), PAIR)
        query = dot(nt_ref[pl.ds(low, block), :cells], gq_ref[:, lanes])
        both = jnp.concatenate([gk_ref[:, lanes], gv_ref[:, lanes]], axis=1)
        return jnp.concatenate([query, dot(nt_ref[pl.ds(low, block), :], both)], axis=1)

    def out_term(half, side, c):
        low = pl.multiple_of((2 * half + side) * block, block)
        columns = out_sums.columns
        return dot(att_t_ref[pl.ds(low, block), :], cot_ref[:, c * columns : (c + 1) * columns])

    split = len(sum_refs) // 2
    qkv_sums.bind(sum_refs[:split], place, qkv_term)
    out_sums.bind(sum_refs[split:], place, out_term)

    loads[0].wait()
    loads[1].wait()
    source = tok_ref[...].astype(f32)
    inverse = lax.rsqrt(jnp.mean(source * source, axis=-1, keepdims=True) + epsilon)
    normed = source * inverse * gain_ref[...]
    own[...] = normed.astype(bf16)
    put_lanes(spread, 0, normed)
    half, block_cells = 2 * ring.block, ring.block
    for at, first_col in ((0, 0), (half, cols - R)):
        for band in range(2):
            low = at + band * block_cells
            strips[low : low + block_cells, :] = strip_blocks(spread, first_col, cols, band * BAND).astype(bf16)
    pl.semaphore_wait(barrier, len(greeted))

    upper = place.lo == 0
    rows16 = lambda at, count: pl.ds(pl.multiple_of(at, 16), count)
    to_above = jnp.where(place.north, TOP, BOTTOM)
    to_below = jnp.where(place.south, BOTTOM, TOP)
    at_above, at_below = to_above * ring.row, to_below * ring.row
    outer_there = jnp.where(upper == place.polar, 0, 3 * block_cells)
    outer_here = jnp.where(upper, 0, block_cells)
    halo_sems, back_sems = (halo_send, halo_recv), (back_send, back_recv)

    def send(src, src_at, dst, dst_at, count, sems, i, j, device):
        return remote(
            src.at[rows16(src_at, count)], dst.at[rows16(dst_at, count)], sems[0].at[i], sems[1].at[j], device
        )

    copies = []
    inner_part = block_cells - outer_here
    for part, sw, se in ((outer_here, WEST, EAST), (inner_part, WEST_LATE, EAST_LATE)):
        copies += [
            send(strips, part, halo, ring.east + block_cells + part, block_cells,
                 halo_sems, sw, se, place.beside_west),
            send(strips, half + part, halo, ring.west + block_cells + part, block_cells,
                 halo_sems, se, sw, place.beside_east),
        ]
    copies += [
        send(own, 0, halo, at_above, ring.row, halo_sems, TOP, to_above, place.above),
        send(own, cells - ring.row, halo, at_below, ring.row, halo_sems, BOTTOM, to_below, place.below),
    ]
    for copy in copies:
        copy.start()
    halo[ring.size :, :] = jnp.zeros((ring.padded - ring.size, width), bf16)
    for ref in (gk_ref, gv_ref):
        ref[cells + ring.size :, :] = jnp.zeros((ring.padded - ring.size, width), bf16)

    tile = CHUNK
    loads[2].wait()
    loads[3].wait()
    for j in range(width // tile):
        at = slice(j * tile, (j + 1) * tile)
        ga_ref[:, at] = dot(cot_ref[...], wout[at, :], NT).astype(bf16)
    loads[4].wait()
    for j in range(width // tile):
        at = slice(j * tile, (j + 1) * tile)
        q_ref[:, at] = dot(own[...], wqkv[:, at]).astype(bf16)

    def keyval(source_ref, low):
        count = source_ref.shape[0]

        def one(j, carry):
            into = pl.ds(pl.multiple_of(j * tile, tile), tile)
            at = pl.ds(pl.multiple_of(width + j * tile, tile), tile)
            kv_ref[low : low + count, into] = dot(source_ref[...], wqkv[:, at]).astype(bf16)
            return carry

        lax.fori_loop(0, 2 * width // tile, one, 0)

    keyval(own, 0)
    nt_ref[:, :cells] = jnp.transpose(own[...])
    window = Window(ring)
    for t in range(window.tiles):
        mask_ref[t] = window.mask(t, place.north, place.south)

    inner_here = jnp.where(upper, 2 * block_cells, block_cells)
    inner_there = jnp.where(upper, 0, 3 * block_cells)

    def arrive(ref, at, count, sems, i):
        piece = ref.at[rows16(at, count)]
        remote(piece, piece, sems[0].at[i], sems[1].at[i], place.sibling).wait_recv()

    here, there = block_cells + outer_here, outer_there
    for i, j, start, from_here, to_there, device in (
        (WEST, OUTER_WEST, ring.west, here, there, place.outer),
        (EAST, OUTER_EAST, ring.east, here, there, place.outer),
        (WEST_LATE, INNER_WEST, ring.west, inner_here, inner_there, place.sibling),
        (EAST_LATE, INNER_EAST, ring.east, inner_here, inner_there, place.sibling),
    ):
        arrive(halo, start + from_here, block_cells, halo_sems, i)
        copy = send(halo, start + from_here, halo, start + to_there, block_cells, halo_sems, j, j, device)
        copy.start()
        copies.append(copy)
    arrive(halo, 0, ring.row, halo_sems, TOP)
    arrive(halo, ring.row, ring.row, halo_sems, BOTTOM)
    outer_own = jnp.where(upper, 0, 3 * block_cells)
    inner_own = jnp.where(upper, 3 * block_cells, 0)
    for i, j, start in ((OUTER_WEST, INNER_WEST, ring.west), (OUTER_EAST, INNER_EAST, ring.east)):
        arrive(halo, start + outer_own, block_cells, halo_sems, i)
        arrive(halo, start + inner_own, block_cells, halo_sems, j)
    keyval(halo, cells)
    nt_ref[:, cells:] = jnp.transpose(halo[...])
    for copy in copies:
        copy.wait_send()

    pairs = width // PAIR

    def attend_pair(pair):
        attend(
            window, pair, width, mask_ref, q_ref, kv_ref, ga_ref, att_ref, att_t_ref, gq_ref, gk_ref, gv_ref
        )
        qkv_sums.step0(pair)

    def step(pair, carry):
        attend_pair(pair)

        @pl.when(pair >= 1)
        def _():
            qkv_sums.step1(pair - 1, lat_first_of(pair - 1))

        @pl.when(pair >= LAG2)
        def _():
            qkv_sums.step2(pair - LAG2, lat_first_of(pair - LAG2))

        @pl.when(pair >= LAG3)
        def _():
            qkv_sums.step3(pair - LAG3, lat_first_of(pair - LAG3))

        return carry

    lax.fori_loop(0, pairs, step, 0)

    outs = out_sums.count
    first_of = lat_first_of
    left2, left3 = list(range(pairs - LAG2, pairs)), list(range(pairs - LAG3, pairs))

    def advance():
        if left2 and (not left3 or left3[0] >= left2[0] - (LAG3 - LAG2)):
            c = left2.pop(0)
            qkv_sums.step2(c, first_of(c))
        elif left3:
            c = left3.pop(0)
            qkv_sums.step3(c, first_of(c))

    qkv_sums.step1(pairs - 1, first_of(pairs - 1))

    def halo_back(j, carry):
        at = pl.ds(pl.multiple_of(j * tile, tile), tile)
        some = slice(cells, cells + ring.size)
        part = dot(gk_ref[some, :], wqkv[at, width : 2 * width], NT)
        stage[:, at] = (part + dot(gv_ref[some, :], wqkv[at, 2 * width :], NT)).astype(bf16)
        return carry

    lax.fori_loop(0, width // tile, halo_back, 0)
    west_at, east_at = 2 * ring.row, 2 * ring.row + half
    outer_west_at, outer_east_at = east_at + half, east_at + half + block_cells
    inner_sent = [
        send(stage, ring.west + inner_own, inner, 0, block_cells, back_sems, INNER_WEST, INNER_WEST, place.sibling),
        send(stage, ring.east + inner_own, inner, block_cells, block_cells,
             back_sems, INNER_EAST, INNER_EAST, place.sibling),
    ]
    ring_sent = inner_sent + [
        send(stage, ring.west + outer_own, back, outer_east_at, block_cells,
             back_sems, OUTER_WEST, OUTER_EAST, place.outer_west),
        send(stage, ring.east + outer_own, back, outer_west_at, block_cells,
             back_sems, OUTER_EAST, OUTER_WEST, place.outer_east),
        send(stage, 0, back, at_above, ring.row, back_sems, TOP, to_above, place.above),
        send(stage, ring.row, back, at_below, ring.row, back_sems, BOTTOM, to_below, place.below),
    ]
    for copy in ring_sent:
        copy.start()
    for c in range(outs):
        out_sums.step0(c)
    for i, j, at, start, there, device in (
        (INNER_WEST, WEST, 0, ring.west, east_at, place.beside_west),
        (INNER_EAST, EAST, block_cells, ring.east, west_at, place.beside_east),
    ):
        arrive(inner, at, block_cells, back_sems, i)
        near = rows16(start + inner_here, block_cells)
        stage[near, :] = (
            stage[near, :].astype(f32) + inner[at : at + block_cells, :].astype(f32)
        ).astype(bf16)
        copy = send(
            stage, start + block_cells, back, there, half, back_sems, j, EAST if j == WEST else WEST, device
        )
        copy.start()
        ring_sent.append(copy)
    for c in range(outs):
        out_sums.step1(c, True)
    for c in range(4):
        advance()

    def own_spread(j, carry):
        at = pl.ds(pl.multiple_of(j * tile, tile), tile)
        part = dot(gq_ref[...], wqkv[at, :width], NT)
        part = part + dot(gk_ref[:cells, :], wqkv[at, width : 2 * width], NT)
        part = part + dot(gv_ref[:cells, :], wqkv[at, 2 * width :], NT)
        put_lanes(spread, j * (tile // LANES), part)
        return carry

    def own_result(j, carry):
        at = pl.ds(pl.multiple_of(j * tile, tile), tile)
        result_ref[:, at] = (dot(att_ref[...], wout[:, at]) + tok_ref[:, at].astype(f32)).astype(bf16)
        return carry

    lax.fori_loop(0, width // tile, own_spread, 0)
    advance()
    advance()
    lax.fori_loop(0, width // tile, own_result, 0)
    stores[0].start()
    while left2:
        advance()
    out_sums.step2(0, True)
    advance()
    for c in range(1, outs):
        out_sums.step2(c, True)
    while left3:
        advance()
    for c in range(outs):
        out_sums.step3(c, True)

    for i, at, count in (
        (TOP, 0, ring.row), (BOTTOM, ring.row, ring.row), (WEST, west_at, half), (EAST, east_at, half),
        (OUTER_WEST, outer_west_at, block_cells), (OUTER_EAST, outer_east_at, block_cells),
    ):
        arrive(back, at, count, back_sems, i)
    came = lambda at, count: back[at : at + count, :].astype(f32)
    groups = width // LANES
    lanes_of = lambda value, g: value[:, g * LANES : (g + 1) * LANES]
    for low, at in ((0, 0), (cells - ring.row, ring.row)):
        rows_back = came(at, ring.row)
        for g in range(groups):
            spread[g, low : low + ring.row, :] += lanes_of(rows_back, g)
    for at, outer_at, first_col in ((west_at, outer_west_at, 0), (east_at, outer_east_at, cols - R)):
        strip, outer = came(at, half), came(outer_at, block_cells)
        for band in range(2):
            here = jnp.where(place.lo == band, outer, 0.0)
            here = here + strip[band * block_cells : (band + 1) * block_cells]
            for c in range(R):
                line = pl.ds(band * BAND * cols + first_col + c, BAND, stride=cols)
                for g in range(groups):
                    spread[g, line, :] += lanes_of(here[c * BAND : (c + 1) * BAND], g)
    grad = jnp.concatenate([spread[g] for g in range(groups)], axis=1)
    scaled = gain_ref[...] * grad
    source = tok_ref[...].astype(f32)
    inverse = lax.rsqrt(jnp.mean(source * source, axis=-1, keepdims=True) + epsilon)
    shift = inverse**3 * jnp.mean(source * scaled, axis=-1, keepdims=True)
    gtok_ref[...] = (cot_ref[...].astype(f32) + inverse * scaled - source * shift).astype(bf16)
    stores[1].start()

    for c in range(pairs):
        total = qkv_sums.step4(c, first_of(c)) * scale
        for kind in range(3):
            low = kind * width + c * PAIR
            gqkv_ref[:, low : low + PAIR] = total[:, kind * PAIR : (kind + 1) * PAIR]
    stores[2].start()
    for c in range(outs):
        columns = out_sums.columns
        gout_ref[:, c * columns : (c + 1) * columns] = out_sums.step4(c, True) * scale
    stores[3].start()
    for copy in ring_sent:
        copy.wait_send()
    for c in range(pairs):
        qkv_sums.drain(c, first_of(c))
    for c in range(outs):
        out_sums.drain(c, True)
    for store in stores:
        store.wait()


def whole_block(ring, lats, lons, scale, tokens, gain, cotangent, w_qkv, w_out):
    cells, width = tokens.shape
    frame = cells + ring.padded
    anywhere = pl.BlockSpec(memory_space=pl.ANY)
    count = 10
    share = width // (lats * lons)
    sems = lambda *shape: pltpu.SemaphoreType.DMA(shape)
    held = lambda *shape: pltpu.VMEM(shape, bf16)
    window = Window(ring)
    qkv_sums = Sums(lats, lons, width, width // PAIR, 3 * PAIR)
    out_sums = Sums(lats, lons, width, width // OUT_COLUMNS, OUT_COLUMNS)
    return pl.pallas_call(
        functools.partial(block_kernel, ring, lats, lons, scale, qkv_sums, out_sums),
        in_specs=[anywhere] * 5,
        out_specs=[anywhere] * 4,
        out_shape=[
            jax.ShapeDtypeStruct((cells, width), bf16),
            jax.ShapeDtypeStruct((cells, width), bf16),
            jax.ShapeDtypeStruct((share, 3 * width), f32),
            jax.ShapeDtypeStruct((share, width), f32),
        ],
        scratch_shapes=[
            held(cells, width), held(cells, width),
            pltpu.VMEM((share, 3 * width), f32), pltpu.VMEM((share, width), f32),
            held(cells, width), pltpu.VMEM(gain.shape, f32), held(cells, width),
            held(*w_qkv.shape), held(*w_out.shape),
            held(cells, width), held(4 * ring.block, width), held(ring.size, width), held(ring.padded, width),
            held(ring.size, width), held(2 * ring.block, width),
            held(cells, width), held(cells, width), held(frame, 2 * width), held(width, frame),
            held(cells, width), held(width, cells), held(cells, width), held(frame, width), held(frame, width),
            pltpu.VMEM((window.tiles, window.keys, 2 * window.queries), f32), pltpu.VMEM((width // LANES, cells, LANES), f32),
            sems(5), sems(4), sems(count), sems(count), sems(count), sems(count),
        ] + qkv_sums.scratch() + out_sums.scratch(),
        compiler_params=pltpu.CompilerParams(
            collective_id=0, has_side_effects=True, vmem_limit_bytes=60 << 20
        ),
        cost_estimate=pl.CostEstimate(
            flops=30 << 30, bytes_accessed=16 << 20, transcendentals=cells * window.keys * H
        ),
    )(tokens, gain, cotangent, w_qkv, w_out)


def deliver(*arrays):
    count = len(arrays)

    def kernel(*refs):
        sources, targets, held = refs[:count], refs[count : 2 * count], refs[2 * count : 3 * count]
        sem_in, sem_out = refs[-2:]
        reads = [pltpu.make_async_copy(sources[i], held[i], sem_in.at[i]) for i in range(count)]
        writes = [pltpu.make_async_copy(held[i], targets[i], sem_out.at[i]) for i in range(count)]
        for read in reads:
            read.start()
        for read, write in zip(reads, writes):
            read.wait()
            write.start()
        for write in writes:
            write.wait()

    anywhere = pl.BlockSpec(memory_space=pl.ANY)
    return pl.pallas_call(
        kernel,
        in_specs=[anywhere] * count,
        out_specs=[anywhere] * count,
        out_shape=[jax.ShapeDtypeStruct(array.shape, array.dtype) for array in arrays],
        scratch_shapes=[pltpu.VMEM(array.shape, array.dtype) for array in arrays]
        + [pltpu.SemaphoreType.DMA((count,))] * 2,
        cost_estimate=pl.CostEstimate(flops=0, bytes_accessed=4 << 20, transcendentals=0),
    )(*arrays)


def shards(tokens, norm_gain, w_qkv, w_out, cotangent):
    rows, cols, width = tokens.shape
    lats, lons = lax.axis_size("lat"), lax.axis_size("lon")
    scale = (rows * cols * lats * lons) ** (-0.5)
    ring = Ring(rows, cols)
    flat = tokens.reshape(-1, width)
    grad_flat = cotangent.reshape(-1, width)
    gain = norm_gain.reshape(1, width)
    result, grad_tokens, grad_qkv, grad_out = deliver(
        *whole_block(ring, lats, lons, scale, flat, gain, grad_flat, w_qkv, w_out)
    )
    return result.reshape(tokens.shape), grad_tokens.reshape(tokens.shape), grad_qkv, grad_out


def solution(mesh):
    placed = (P("lat", "lon", None), P(), P(), P(), P("lat", "lon", None))
    return jax.shard_map(
        shards,
        mesh=mesh,
        in_specs=placed,
        out_specs=(
            P("lat", "lon", None),
            P("lat", "lon", None),
            P(("lat", "lon"), None),
            P(("lat", "lon"), None),
        ),
        check_vma=False,
    )
```
